32 devices in a mesh: ctx: 16 (over z, y, core), fsdp: 2 (over x).
Axes of the slice: x: 2, y: 2, z: 4, core: 2. Of those that a mesh axis runs over, the one named last changes fastest.
Arguments:
- layer_input: float32 [4096, 1024], P(('ctx', 'fsdp')), may hold values from -6 to 6
- grad_output: float32 [4096, 1024], P(('ctx', 'fsdp')), may hold values from -6 to 6
- positions: int32 [4096], replicated, may hold values from 0 to 4095, as said below
- w_query: bfloat16 [1024, 2048], P(('ctx', 'fsdp')), may hold values from -0.1875 to 0.1875
- w_key: bfloat16 [1024, 2048], P(('ctx', 'fsdp')), may hold values from -0.1875 to 0.1875
- w_value: bfloat16 [1024, 2048], P(('ctx', 'fsdp')), may hold values from -0.1875 to 0.1875
- w_out: bfloat16 [2048, 1024], P(('ctx', 'fsdp')), may hold values from -0.125 to 0.125
- w_gate: bfloat16 [1024, 4096], P(('ctx', 'fsdp')), may hold values from -0.1875 to 0.1875
- w_up: bfloat16 [1024, 4096], P(('ctx', 'fsdp')), may hold values from -0.1875 to 0.1875
- w_down: bfloat16 [4096, 1024], P(('ctx', 'fsdp')), may hold values from -0.09375 to 0.09375
- gain_query: bfloat16 [2048], P(('ctx', 'fsdp')), may hold values from 0.5 to 1.5
- gain_key: bfloat16 [2048], P(('ctx', 'fsdp')), may hold values from 0.5 to 1.5
- gain_attn: bfloat16 [1024], P(('ctx', 'fsdp')), may hold values from 0.5 to 1.5
- gain_mlp: bfloat16 [1024], P(('ctx', 'fsdp')), may hold values from 0.5 to 1.5
Outputs:
- output: float32 [4096, 1024], P(('ctx', 'fsdp'))
- grad_input: float32 [4096, 1024], P(('ctx', 'fsdp'))
- grad_w_query: float32 [1024, 2048], P('fsdp')
- grad_w_key: float32 [1024, 2048], P('fsdp')
- grad_w_value: float32 [1024, 2048], P('fsdp')
- grad_w_out: float32 [2048, 1024], P('fsdp')
- grad_w_gate: float32 [1024, 4096], P('fsdp')
- grad_w_up: float32 [1024, 4096], P('fsdp')
- grad_w_down: float32 [4096, 1024], P('fsdp')
- grad_gain_query: float32 [2048], P('fsdp')
- grad_gain_key: float32 [2048], P('fsdp')
- grad_gain_attn: float32 [1024], P('fsdp')
- grad_gain_mlp: float32 [1024], P('fsdp')
The draws below stay inside these ranges and needn't reach their ends.
Inputs may be any that keep to these rules, and one draw needn't show every extreme that they name: positions holds each of 0 to 4095 once. The 128 rows of device d (rows d * 128 onward, devices in the order ctx then fsdp) are two sequence blocks of 64 consecutive positions: block p first and block 63 - p second, for some p below 32 that differs from device to device.
All inputs are finite; a program needn't handle non-finite values.
Results may differ from the reference program's by a relative error of at most 0.023.
Values may be sent and summed in bfloat16 or wider, within the bound.
No kernel may reach another device: no remote copies, remote signals or barrier semaphores. Data moves between devices by JAX's collectives and lax.ppermute only.
A program may use at most 768 MiB of HBM per device.

```python
import math
import jax
import jax.numpy as jnp
from jax import lax

D = 1024
H = 16
HD = 128
F = 4096
E = 2048
BLK = 64
BLOCKS = 64
SEQ = 4096


def draw_positions(key, part):
    pairs = BLOCKS // 2
    order = jax.random.permutation(key, pairs).astype(jnp.int32)
    blocks = jnp.stack([order, BLOCKS - 1 - order], axis=1).reshape(-1)
    offsets = jnp.arange(BLK, dtype=jnp.int32)
    return (blocks[:, None] * BLK + offsets[None, :]).reshape(-1).astype(jnp.int32)


def level_of(own_key, dims, cuts, low, top_value):
    loudness = 1.0
    for position, parts in cuts:
        steps = jax.random.uniform(jax.random.fold_in(jax.random.fold_in(own_key, 6), position), (parts,), jnp.float32, low / len(cuts), top_value / len(cuts))
        loudness = loudness * jnp.repeat(jnp.exp(steps), dims[position] // parts).reshape((-1,) + (1,) * (len(dims) - 1 - position))
    return loudness


def bell_draw(own_key, extent, spread, limit, cuts=(), kind=jnp.bfloat16):
    entries = jax.random.normal(own_key, extent, jnp.float32) * spread
    if len(cuts) > 0:
        entries = level_of(own_key, extent, cuts, -0.22, 0.18) * entries
    return jnp.clip(entries, min=-limit, max=limit).astype(kind)


def setup_inputs(seed: int = 0) -> dict:
    key_list = jax.random.split(jax.random.key(seed), 15)
    return {
        "layer_input": bell_draw(key_list[0], (SEQ, D), 1.0, 6.0, ((0, 32),), jnp.float32),
        "grad_output": bell_draw(key_list[1], (SEQ, D), 1.0, 6.0, ((0, 32),), jnp.float32),
        "positions": draw_positions(jax.random.fold_in(key_list[14], 71), 0),
        "w_query": bell_draw(key_list[3], (D, E), D ** -0.5, 0.1875, ((0, 32),)),
        "w_key": bell_draw(key_list[4], (D, E), D ** -0.5, 0.1875, ((0, 32),)),
        "w_value": bell_draw(key_list[5], (D, E), D ** -0.5, 0.1875, ((0, 32),)),
        "w_out": bell_draw(key_list[6], (E, D), E ** -0.5, 0.125, ((0, 32),)),
        "w_gate": bell_draw(key_list[7], (D, F), D ** -0.5, 0.1875, ((0, 32),)),
        "w_up": bell_draw(key_list[8], (D, F), D ** -0.5, 0.1875, ((0, 32),)),
        "w_down": bell_draw(key_list[9], (F, D), F ** -0.5, 0.09375, ((0, 32),)),
        "gain_query": jnp.clip(1.0 + 0.1 * jax.random.normal(key_list[10], (E,), jnp.float32), 0.5, 1.5).astype(jnp.bfloat16),
        "gain_key": jnp.clip(1.0 + 0.1 * jax.random.normal(key_list[11], (E,), jnp.float32), 0.5, 1.5).astype(jnp.bfloat16),
        "gain_attn": jnp.clip(1.0 + 0.1 * jax.random.normal(key_list[12], (D,), jnp.float32), 0.5, 1.5).astype(jnp.bfloat16),
        "gain_mlp": jnp.clip(1.0 + 0.1 * jax.random.normal(key_list[13], (D,), jnp.float32), 0.5, 1.5).astype(jnp.bfloat16),
    }


EPS = 1e-06
THETA = 500000.0
NEG = -1e+30

def norm_forward(value, gain):
    recip = lax.rsqrt(lax.optimization_barrier(jnp.mean(value * value, axis=-1, keepdims=True)) + EPS)
    return (value * recip * gain.astype(jnp.float32), recip)

def norm_backward(value, recip, gain, grad_out):
    scaled = grad_out * gain.astype(jnp.float32)
    width = value.shape[-1]
    grad_in = recip * scaled - value * (recip * recip * recip) * lax.optimization_barrier(jnp.sum(scaled * value, axis=-1, keepdims=True)) / width
    grad_gain = lax.optimization_barrier(jnp.sum(grad_out * value * recip, axis=0))
    return (grad_in, grad_gain)

def rotary_tables(where, head_size):
    half = head_size // 2
    freqs = THETA ** (-(2.0 * jnp.arange(half, dtype=jnp.float32)) / head_size)
    angles = where.astype(jnp.float32)[:, None] * freqs[None, :]
    return (jnp.cos(angles)[:, None, :], jnp.sin(angles)[:, None, :])

def rotate(flat, cosine, sine, heads, head_size):
    half = head_size // 2
    table = flat.reshape(flat.shape[0], heads, head_size)
    first = table[..., :half]
    second = table[..., half:]
    joined = jnp.concatenate([first * cosine - second * sine, second * cosine + first * sine], axis=-1)
    return joined.reshape(flat.shape[0], heads * head_size)

def unrotate(flat, cosine, sine, heads, head_size):
    half = head_size // 2
    table = flat.reshape(flat.shape[0], heads, head_size)
    first = table[..., :half]
    second = table[..., half:]
    joined = jnp.concatenate([first * cosine + second * sine, second * cosine - first * sine], axis=-1)
    return joined.reshape(flat.shape[0], heads * head_size)

def reference(layer_input, grad_output, positions, w_query, w_key, w_value, w_out, w_gate, w_up, w_down, gain_query, gain_key, gain_attn, gain_mlp):
    f32 = jnp.float32
    bf16 = jnp.bfloat16
    order = jnp.zeros((SEQ,), jnp.int32).at[positions].set(jnp.arange(SEQ, dtype=jnp.int32))
    xs = layer_input[order]
    gs = grad_output[order]
    seq_pos = jnp.arange(SEQ, dtype=jnp.int32)
    cosine, sine = rotary_tables(seq_pos, HD)
    scale = 1.0 / math.sqrt(HD)
    xb = xs.astype(bf16)
    query_pre = jnp.dot(xb, w_query, preferred_element_type=f32)
    key_pre = jnp.dot(xb, w_key, preferred_element_type=f32)
    query_normed, q_recip = norm_forward(query_pre, gain_query)
    key_normed, k_recip = norm_forward(key_pre, gain_key)
    query = rotate(query_normed, cosine, sine, H, HD).astype(bf16)
    key = rotate(key_normed, cosine, sine, H, HD).astype(bf16)
    value = jnp.dot(xb, w_value, preferred_element_type=f32).astype(bf16)
    q3 = query.reshape(SEQ, H, HD).astype(f32)
    k3 = key.reshape(SEQ, H, HD).astype(f32)
    v3 = value.reshape(SEQ, H, HD).astype(f32)
    qblk = min(512, SEQ)
    nblk = SEQ // qblk
    pieces = []
    lses = []
    for blk in range(nblk):
        low = blk * qblk
        high = low + qblk
        scores = jnp.einsum('qhd,khd->hqk', q3[low:high], k3[:high]) * scale
        allowed = jnp.arange(high, dtype=jnp.int32)[None, None, :] <= jnp.arange(low, high, dtype=jnp.int32)[None, :, None]
        scores = jnp.where(allowed, scores, NEG)
        top = lax.optimization_barrier(jnp.max(scores, axis=-1, keepdims=True))
        total = lax.optimization_barrier(jnp.sum(jnp.where(allowed, jnp.exp(scores - top), 0.0), axis=-1, keepdims=True))
        lse = top + jnp.log(total)
        weights = jnp.where(allowed, jnp.exp(scores - lse), 0.0).astype(bf16)
        pieces.append(jnp.einsum('hqk,khd->qhd', weights.astype(f32), v3[:high]))
        lses.append(lse[:, :, 0])
    attended = jnp.concatenate(pieces, axis=0).reshape(SEQ, E).astype(bf16)
    proj = jnp.dot(attended, w_out, preferred_element_type=f32)
    attn_branch, a_recip = norm_forward(proj, gain_attn)
    mid = xs + attn_branch
    midb = mid.astype(bf16)
    gate = jnp.dot(midb, w_gate, preferred_element_type=f32)
    up = jnp.dot(midb, w_up, preferred_element_type=f32)
    sig = jax.nn.sigmoid(gate)
    silu = gate * sig
    hidden = (silu * up).astype(bf16)
    down = jnp.dot(hidden, w_down, preferred_element_type=f32)
    mlp_branch, m_recip = norm_forward(down, gain_mlp)
    output = mid + mlp_branch
    d_down_f, grad_gain_mlp = norm_backward(down, m_recip, gain_mlp, gs)
    d_down = d_down_f.astype(bf16)
    grad_w_down = jnp.dot(hidden.T, d_down, preferred_element_type=f32)
    d_hidden = jnp.dot(d_down, w_down.T, preferred_element_type=f32)
    d_gate = (d_hidden * up * sig * (1.0 + gate * (1.0 - sig))).astype(bf16)
    d_up = (d_hidden * silu).astype(bf16)
    grad_w_gate = jnp.dot(midb.T, d_gate, preferred_element_type=f32)
    grad_w_up = jnp.dot(midb.T, d_up, preferred_element_type=f32)
    d_mid = gs + jnp.dot(d_gate, w_gate.T, preferred_element_type=f32) + jnp.dot(d_up, w_up.T, preferred_element_type=f32)
    d_proj_f, grad_gain_attn = norm_backward(proj, a_recip, gain_attn, d_mid)
    d_proj = d_proj_f.astype(bf16)
    grad_w_out = jnp.dot(attended.T, d_proj, preferred_element_type=f32)
    d_att = jnp.dot(d_proj, w_out.T, preferred_element_type=f32).astype(bf16)
    da3 = d_att.reshape(SEQ, H, HD).astype(f32)
    delta = lax.optimization_barrier(jnp.sum(da3 * attended.reshape(SEQ, H, HD).astype(f32), axis=-1))
    dq_parts = []
    dk_acc = jnp.zeros((SEQ, H, HD), f32)
    dv_acc = jnp.zeros((SEQ, H, HD), f32)
    for blk in range(nblk):
        low = blk * qblk
        high = low + qblk
        scores = jnp.einsum('qhd,khd->hqk', q3[low:high], k3[:high]) * scale
        allowed = jnp.arange(high, dtype=jnp.int32)[None, None, :] <= jnp.arange(low, high, dtype=jnp.int32)[None, :, None]
        prob = jnp.where(allowed, jnp.exp(scores - lses[blk][:, :, None]), 0.0)
        weights = prob.astype(bf16).astype(f32)
        dprob = jnp.einsum('qhd,khd->hqk', da3[low:high], v3[:high])
        dscore = (prob * (dprob - delta[low:high].T[:, :, None])).astype(bf16).astype(f32)
        dq_parts.append(jnp.einsum('hqk,khd->qhd', dscore, k3[:high]) * scale)
        dk_acc = dk_acc.at[:high].add(jnp.einsum('hqk,qhd->khd', dscore, q3[low:high]) * scale)
        dv_acc = dv_acc.at[:high].add(jnp.einsum('hqk,qhd->khd', weights, da3[low:high]))
    d_query_rot = jnp.concatenate(dq_parts, axis=0).reshape(SEQ, E)
    d_key_rot = dk_acc.reshape(SEQ, E)
    d_value = dv_acc.reshape(SEQ, E).astype(bf16)
    dq_f, grad_gain_query = norm_backward(query_pre, q_recip, gain_query, unrotate(d_query_rot, cosine, sine, H, HD))
    dk_f, grad_gain_key = norm_backward(key_pre, k_recip, gain_key, unrotate(d_key_rot, cosine, sine, H, HD))
    d_query_pre = dq_f.astype(bf16)
    d_key_pre = dk_f.astype(bf16)
    grad_w_query = jnp.dot(xb.T, d_query_pre, preferred_element_type=f32)
    grad_w_key = jnp.dot(xb.T, d_key_pre, preferred_element_type=f32)
    grad_w_value = jnp.dot(xb.T, d_value, preferred_element_type=f32)
    grad_input = d_mid + jnp.dot(d_query_pre, w_query.T, preferred_element_type=f32) + jnp.dot(d_key_pre, w_key.T, preferred_element_type=f32) + jnp.dot(d_value, w_value.T, preferred_element_type=f32)
    return (output[positions], grad_input[positions], grad_w_query, grad_w_key, grad_w_value, grad_w_out, grad_w_gate, grad_w_up, grad_w_down, grad_gain_query, grad_gain_key, grad_gain_attn, grad_gain_mlp)
```

```python
import functools
import math

import jax
import jax.numpy as jnp
from jax import lax
from jax.experimental import pallas as pl
from jax.experimental.pallas import tpu as pltpu
from jax.sharding import Mesh
from jax.sharding import PartitionSpec as P

NEG = -1e30


def dot(a, b, ca, cb):
    return lax.dot_general(a, b, (((ca,), (cb,)), ((), ())), preferred_element_type=jnp.float32)


def query_positions(seq_ref, tile, per, blk):
    lane = lax.broadcasted_iota(jnp.int32, (1, per * blk), 1)
    out = jnp.zeros((1, per * blk), jnp.int32)
    for b in range(per):
        first = seq_ref[tile * per + b] * blk
        out = jnp.where(lane // blk == b, first + lane - b * blk, out)
    return out


def sorted_load(src, dst, sem, count, blk, slot):
    def start(i, carry):
        pltpu.make_async_copy(
            src.at[pl.ds(pl.multiple_of(i * blk, blk), blk), :],
            dst.at[pl.ds(pl.multiple_of(slot(i) * blk, blk), blk), :],
            sem,
        ).start()
        return carry

    lax.fori_loop(0, count, start, 0)


def attend_kernel(
    place_ref, seq_ref, kslot_ref, q_ref, kv_ref, o_ref, lse_ref, q_s, kv_s, o_s, sems,
    *, heads, head_size, blk, per, chunk, scale
):
    nq = q_s.shape[0] // blk
    nk = kv_s.shape[0] // blk
    width = heads * head_size
    rows = per * blk
    sorted_load(q_ref, q_s, sems.at[0], nq, blk, lambda i: place_ref[i])
    sorted_load(kv_ref, kv_s, sems.at[1], nk, blk, lambda i: kslot_ref[i])
    pltpu.make_async_copy(q_ref, q_s, sems.at[0]).wait()
    pltpu.make_async_copy(kv_ref, kv_s, sems.at[1]).wait()

    def tile_body(tile, carry):
        base = pl.multiple_of(tile * rows, rows)
        qpos = query_positions(seq_ref, tile, per, blk)
        full = (seq_ref[tile * per] * blk) // chunk
        last = ((seq_ref[tile * per + per - 1] + 1) * blk + chunk - 1) // chunk
        for h in range(heads):
            cols = pl.ds(h * head_size, head_size)
            vcols = pl.ds(width + h * head_size, head_size)
            qt = q_s[pl.ds(base, rows), cols]

            def step(j, state, masked):
                top, total, acc = state
                low = pl.multiple_of(j * chunk, chunk)
                s = dot(kv_s[pl.ds(low, chunk), cols], qt, 1, 1) * scale
                if masked:
                    kpos = low + lax.broadcasted_iota(jnp.int32, s.shape, 0)
                    s = jnp.where(kpos <= qpos, s, NEG)
                top_new = jnp.maximum(top, jnp.max(s, axis=0, keepdims=True))
                p = jnp.exp(s - top_new)
                factor = jnp.exp(top - top_new)
                total = total * factor + jnp.sum(p, axis=0, keepdims=True)
                acc = acc * factor + dot(kv_s[pl.ds(low, chunk), vcols], p.astype(jnp.bfloat16), 0, 0)
                return top_new, total, acc

            state = (
                jnp.full((1, rows), NEG, jnp.float32),
                jnp.zeros((1, rows), jnp.float32),
                jnp.zeros((head_size, rows), jnp.float32),
            )
            state = lax.fori_loop(0, full, functools.partial(step, masked=False), state)
            top, total, acc = lax.fori_loop(full, last, functools.partial(step, masked=True), state)
            o_s[pl.ds(base, rows), cols] = (acc / total).T.astype(o_s.dtype)
            lse_ref[pl.ds(tile * heads + h, 1), :] = top + jnp.log(total)
        return carry

    lax.fori_loop(0, nq // per, tile_body, 0)

    def put(i, carry):
        pltpu.make_async_copy(
            o_s.at[pl.ds(pl.multiple_of(place_ref[i] * blk, blk), blk), :],
            o_ref.at[pl.ds(pl.multiple_of(i * blk, blk), blk), :],
            sems.at[0],
        ).start()
        return carry

    lax.fori_loop(0, nq, put, 0)
    pltpu.make_async_copy(o_s, o_ref, sems.at[0]).wait()


def attend(place, seq, kslot, q, kv, heads, head_size, blk):
    nq = q.shape[0] // blk
    per = min(4, nq)
    chunk = 512
    rows = per * blk
    width = heads * head_size
    scale = 1.0 / math.sqrt(head_size)
    return pl.pallas_call(
        functools.partial(
            attend_kernel, heads=heads, head_size=head_size, blk=blk, per=per, chunk=chunk, scale=scale
        ),
        out_shape=(
            jax.ShapeDtypeStruct(q.shape, q.dtype),
            jax.ShapeDtypeStruct((nq // per * heads, rows), jnp.float32),
        ),
        grid_spec=pltpu.PrefetchScalarGridSpec(
            num_scalar_prefetch=3,
            grid=(),
            in_specs=[pl.BlockSpec(memory_space=pl.ANY)] * 2,
            out_specs=[pl.BlockSpec(memory_space=pl.ANY), pl.BlockSpec(memory_space=pltpu.VMEM)],
            scratch_shapes=[
                pltpu.VMEM(q.shape, q.dtype),
                pltpu.VMEM(kv.shape, kv.dtype),
                pltpu.VMEM(q.shape, q.dtype),
                pltpu.SemaphoreType.DMA((2,)),
            ],
        ),
        compiler_params=pltpu.CompilerParams(vmem_limit_bytes=56 * 1024 * 1024),
        name="attend",
    )(place, seq, kslot, q, kv)


def attend_back_kernel(
    place_ref, seq_ref, kslot_ref, q_ref, kv_ref, o_ref, do_ref, lse_ref,
    dq_ref, dkv_ref, q_s, kv_s, o_s, do_s, dq_s, dkv_s, sems,
    *, heads, head_size, blk, per, chunk, scale
):
    nq = q_s.shape[0] // blk
    nk = kv_s.shape[0] // blk
    width = heads * head_size
    rows = per * blk
    sorted_load(q_ref, q_s, sems.at[0], nq, blk, lambda i: place_ref[i])
    sorted_load(o_ref, o_s, sems.at[1], nq, blk, lambda i: place_ref[i])
    sorted_load(do_ref, do_s, sems.at[2], nq, blk, lambda i: place_ref[i])
    sorted_load(kv_ref, kv_s, sems.at[3], nk, blk, lambda i: kslot_ref[i])
    dkv_s[...] = jnp.zeros_like(dkv_s)
    pltpu.make_async_copy(q_ref, q_s, sems.at[0]).wait()
    pltpu.make_async_copy(o_ref, o_s, sems.at[1]).wait()
    pltpu.make_async_copy(do_ref, do_s, sems.at[2]).wait()
    pltpu.make_async_copy(kv_ref, kv_s, sems.at[3]).wait()

    def tile_body(tile, carry):
        base = pl.multiple_of(tile * rows, rows)
        qpos = query_positions(seq_ref, tile, per, blk)
        full = (seq_ref[tile * per] * blk) // chunk
        last = ((seq_ref[tile * per + per - 1] + 1) * blk + chunk - 1) // chunk
        for h in range(heads):
            cols = pl.ds(h * head_size, head_size)
            vcols = pl.ds(width + h * head_size, head_size)
            qt = q_s[pl.ds(base, rows), cols]
            dot_o = do_s[pl.ds(base, rows), cols]
            prod = dot_o.astype(jnp.float32) * o_s[pl.ds(base, rows), cols].astype(jnp.float32)
            delta = jnp.sum(prod.T, axis=0, keepdims=True)
            lse = lse_ref[pl.ds(tile * heads + h, 1), :]

            def step(j, acc, masked):
                low = pl.multiple_of(j * chunk, chunk)
                krows = pl.ds(low, chunk)
                kc = kv_s[krows, cols]
                s = dot(kc, qt, 1, 1) * scale - lse
                if masked:
                    kpos = low + lax.broadcasted_iota(jnp.int32, s.shape, 0)
                    s = jnp.where(kpos <= qpos, s, NEG)
                p = jnp.exp(s)
                dp = dot(kv_s[krows, vcols], dot_o, 1, 1)
                ds = (p * (dp - delta)).astype(jnp.bfloat16)
                dkv_s[krows, vcols] += dot(p.astype(jnp.bfloat16), dot_o, 1, 0)
                dkv_s[krows, cols] += dot(ds, qt, 1, 0)
                return acc + dot(kc, ds, 0, 0)

            acc = jnp.zeros((head_size, rows), jnp.float32)
            acc = lax.fori_loop(0, full, functools.partial(step, masked=False), acc)
            acc = lax.fori_loop(full, last, functools.partial(step, masked=True), acc)
            dq_s[pl.ds(base, rows), cols] = (acc * scale).T.astype(dq_s.dtype)
        return carry

    lax.fori_loop(0, nq // per, tile_body, 0)
    kv_s[:, :width] = (dkv_s[:, :width] * scale).astype(kv_s.dtype)
    kv_s[:, width:] = dkv_s[:, width:].astype(kv_s.dtype)

    def put_q(i, carry):
        pltpu.make_async_copy(
            dq_s.at[pl.ds(pl.multiple_of(place_ref[i] * blk, blk), blk), :],
            dq_ref.at[pl.ds(pl.multiple_of(i * blk, blk), blk), :],
            sems.at[0],
        ).start()
        return carry

    def put_k(i, carry):
        pltpu.make_async_copy(
            kv_s.at[pl.ds(pl.multiple_of(kslot_ref[i] * blk, blk), blk), :],
            dkv_ref.at[pl.ds(pl.multiple_of(i * blk, blk), blk), :],
            sems.at[3],
        ).start()
        return carry

    lax.fori_loop(0, nq, put_q, 0)
    lax.fori_loop(0, nk, put_k, 0)
    pltpu.make_async_copy(dq_s, dq_ref, sems.at[0]).wait()
    pltpu.make_async_copy(kv_s, dkv_ref, sems.at[3]).wait()


def attend_back(place, seq, kslot, q, kv, o, do, lse, heads, head_size, blk):
    nq = q.shape[0] // blk
    per = min(4, nq)
    chunk = 512
    scale = 1.0 / math.sqrt(head_size)
    return pl.pallas_call(
        functools.partial(
            attend_back_kernel, heads=heads, head_size=head_size, blk=blk, per=per, chunk=chunk, scale=scale
        ),
        out_shape=(
            jax.ShapeDtypeStruct(q.shape, jnp.float32),
            jax.ShapeDtypeStruct(kv.shape, kv.dtype),
        ),
        grid_spec=pltpu.PrefetchScalarGridSpec(
            num_scalar_prefetch=3,
            grid=(),
            in_specs=[pl.BlockSpec(memory_space=pl.ANY)] * 4 + [pl.BlockSpec(memory_space=pltpu.VMEM)],
            out_specs=[pl.BlockSpec(memory_space=pl.ANY)] * 2,
            scratch_shapes=[
                pltpu.VMEM(q.shape, q.dtype),
                pltpu.VMEM(kv.shape, kv.dtype),
                pltpu.VMEM(q.shape, q.dtype),
                pltpu.VMEM(q.shape, q.dtype),
                pltpu.VMEM(q.shape, jnp.float32),
                pltpu.VMEM(kv.shape, jnp.float32),
                pltpu.SemaphoreType.DMA((4,)),
            ],
        ),
        compiler_params=pltpu.CompilerParams(vmem_limit_bytes=58 * 1024 * 1024),
        name="attend_back",
    )(place, seq, kslot, q, kv, o, do, lse)


EPS = 1e-06
THETA = 500000.0
HD = 128


def norm_forward(value, gain):
    recip = lax.rsqrt(jnp.mean(value * value, axis=-1, keepdims=True) + EPS)
    return (value * recip * gain, recip)


def norm_backward(value, recip, gain, grad_out):
    scaled = grad_out * gain
    width = value.shape[-1]
    grad_in = (
        recip * scaled
        - value * (recip * recip * recip) * jnp.sum(scaled * value, axis=-1, keepdims=True) / width
    )
    grad_gain = jnp.sum(grad_out * value * recip, axis=0)
    return (grad_in, grad_gain)


def turn(flat, cosine, sine, heads):
    half = HD // 2
    table = flat.reshape(flat.shape[0], heads, HD)
    first = table[..., :half]
    second = table[..., half:]
    joined = jnp.concatenate(
        [first * cosine - second * sine, second * cosine + first * sine], axis=-1
    )
    return joined.reshape(flat.shape[0], heads * HD)


def flip(value, *axes):
    last = 2 ** len(axes) - 1
    return lax.ppermute(value, axes, [(i, i ^ last) for i in range(last + 1)])


def gather8(x, a, b):
    mine = jnp.stack([x, flip(x, b), flip(x, a), flip(x, a, b)])
    other = flip(mine, "c")
    return jnp.concatenate([mine, other]).reshape(8 * x.shape[0], x.shape[1])


def scatter8(x, a, b):
    bf16 = jnp.bfloat16
    parts = x.astype(bf16).reshape(2, 4, x.shape[0] // 8, x.shape[1])
    mine = x.reshape(parts.shape)[0] + flip(parts[1], "c").astype(jnp.float32)
    out = mine.astype(bf16)
    return (
        mine[0]
        + flip(out[1], b).astype(jnp.float32)
        + flip(out[2], a).astype(jnp.float32)
        + flip(out[3], a, b).astype(jnp.float32)
    )


def sum8(x, a, b):
    t = x.reshape((2, 2, 2) + x.shape[1:])
    for axis, name in enumerate(("c", a, b)):
        t = t + jnp.flip(flip(t, name), axis)
    return t.reshape(x.shape)


def in_order(value, axis, name):
    return jnp.where(lax.axis_index(name) == 1, jnp.flip(value, axis), value)


def gather4(x, a, b):
    pair = jnp.stack([x, flip(x, a)])
    quad = jnp.stack([pair, flip(pair, b)])
    return in_order(in_order(quad, 1, a), 0, b)


def halve(x, name):
    me = lax.axis_index(name)
    keep = lax.dynamic_index_in_dim(x, me, 0, keepdims=False)
    send = lax.dynamic_index_in_dim(x, 1 - me, 0, keepdims=False)
    return keep.astype(jnp.float32) + flip(send.astype(jnp.bfloat16), name).astype(jnp.float32)


def spread(x, a, b):
    pair = jnp.stack([x, flip(x, a)])
    return jnp.stack([pair, flip(pair, b)])


def collect(x, a, b):
    half = x[0].astype(jnp.float32) + flip(x[1], b).astype(jnp.float32)
    return half[0] + flip(half[1].astype(jnp.bfloat16), a).astype(jnp.float32)


def layer(
    layer_input,
    grad_output,
    positions,
    w_query,
    w_key,
    w_value,
    w_out,
    w_gate,
    w_up,
    w_down,
    gain_query,
    gain_key,
    gain_attn,
    gain_mlp,
    *,
    outer,
):
    f32 = jnp.float32
    bf16 = jnp.bfloat16
    rows, d = layer_input.shape
    drows, e = w_query.shape
    f = w_gate.shape[1]
    blk = rows // 2
    devices = positions.shape[0] // rows
    teams = devices // 8
    every = ("o", "h", "l", "y", "c", "x")
    heads = e // HD
    mine = heads // 8
    wide = mine * HD
    index = {name: lax.axis_index(name) for name in every}

    aligned = w_out.shape[0] * teams == wide and outer == 1 and (wide // mine) == 2 * w_out.shape[0]
    if aligned:
        def by_team(w):
            return w.reshape(drows, 4, 2, 2, HD).transpose(1, 3, 0, 2, 4).reshape(8, drows, wide)
    else:
        def by_team(w):
            return w.reshape(drows, 8, wide).transpose(1, 0, 2)

    gains = jnp.concatenate([gain_query, gain_key, gain_attn, gain_mlp])
    pad = drows * 128 - gains.shape[0]
    gains = jnp.pad(gains, (0, pad)).reshape(1, drows, 128)
    payload = jnp.concatenate(
        [by_team(w_query), by_team(w_key), by_team(w_value), jnp.broadcast_to(gains, (8, drows, 128))],
        axis=2,
    )
    payload = lax.all_to_all(payload, ("h", "l", "c"), 0, 0, tiled=True)
    payload = gather4(payload, "y", "x")
    if outer > 1:
        payload = lax.all_gather(payload, "o", axis=0)
    else:
        payload = payload[None]
    payload = payload.reshape(outer, 2, 2, 2, 2, 2, drows, 3 * wide + 128)
    payload = payload.transpose(0, 3, 4, 2, 5, 1, 6, 7).reshape(d, 3 * wide + 128)
    w_qkv = payload[:, : 3 * wide]
    gains = payload[:, 3 * wide :].reshape(devices, drows * 128)
    e_own, d_own = e // devices, d // devices
    full_gq = gains[:, :e_own].reshape(e)
    full_gk = gains[:, e_own : 2 * e_own].reshape(e)
    full_ga = gains[:, 2 * e_own : 2 * e_own + d_own].reshape(1, d).astype(f32)
    full_gm = gains[:, 2 * e_own + d_own : 2 * e_own + 2 * d_own].reshape(1, d).astype(f32)
    team_a = index["h"] * 4 + index["l"] * 2 + index["c"]
    if aligned:
        def own_gain(g):
            t = g.reshape(4, 2, 2, HD).transpose(0, 2, 1, 3).reshape(8, wide)
            return lax.dynamic_slice_in_dim(t, team_a, 1, 0).astype(f32)
    else:
        def own_gain(g):
            return lax.dynamic_slice_in_dim(g.reshape(8, wide), team_a, 1, 0).astype(f32)
    gq, gk = own_gain(full_gq), own_gain(full_gk)

    if aligned:
        w_o = gather4(w_out, "x", "y").reshape(wide, d)
    else:
        w_o = lax.all_gather(w_out, every, axis=0, tiled=True)
        w_o = lax.dynamic_slice_in_dim(w_o, team_a * wide, wide, 0)

    unit = f // (8 * outer * 2)
    units = outer * 2 * unit

    def by_unit(w):
        return w.reshape(drows, outer * 2, 8, unit).transpose(2, 0, 1, 3).reshape(8, drows, units)

    ff = jnp.concatenate([by_unit(w_gate), by_unit(w_up)], axis=2)
    ff = lax.all_to_all(ff, ("l", "y", "c"), 0, 0, tiled=True)
    ff = gather4(ff, "h", "x")
    w_d = gather4(w_down, "h", "x")
    if outer > 1:
        ff = lax.all_gather(ff, "o", axis=0)
        w_d = lax.all_gather(w_d, "o", axis=0)
    else:
        ff, w_d = ff[None], w_d[None]
    ff = ff.reshape(outer, 2, 2, 2, 2, 2, drows, 2 * units)
    w_gu = ff.transpose(0, 2, 3, 4, 5, 1, 6, 7).reshape(d, 2 * units)
    w_d = w_d.transpose(0, 2, 1, 3, 4).reshape(units, d)

    table = positions.reshape(outer, 2, 2, 2, 2, 2, rows)[..., ::blk] // blk
    for axis, name in enumerate(every):
        if name != "o":
            table = in_order(table, axis, name)
    kslot = table.transpose(0, 5, 3, 4, 1, 2, 6)
    qblocks = lax.dynamic_index_in_dim(kslot, index["o"], 0, keepdims=False)[0, 0].reshape(-1)
    kslot = kslot.reshape(-1)
    nq = qblocks.shape[0]
    place = jnp.sum((qblocks[None, :] < qblocks[:, None]).astype(jnp.int32), axis=1)
    seq = jnp.sum(
        jnp.where(place[None, :] == jnp.arange(nq)[:, None], qblocks[None, :], 0), axis=1
    ).astype(jnp.int32)
    group_pos = (qblocks[:, None] * blk + jnp.arange(blk, dtype=jnp.int32)[None, :]).reshape(-1)
    freqs = THETA ** (-(2.0 * jnp.arange(HD // 2, dtype=f32)) / HD)
    angles = group_pos.astype(f32)[:, None] * freqs[None, :]
    cosine, sine = jnp.cos(angles)[:, None, :], jnp.sin(angles)[:, None, :]

    xg = gather8(layer_input.astype(bf16), "h", "l")
    group = xg.shape[0]
    pre = jnp.dot(xg, w_qkv, preferred_element_type=f32)
    q_pre, k_pre, value = pre[:, :wide], pre[:, wide : 2 * wide], pre[:, 2 * wide :].astype(bf16)
    squares = jnp.stack([jnp.sum(q_pre * q_pre, axis=-1), jnp.sum(k_pre * k_pre, axis=-1)])
    squares = sum8(squares.reshape(2, 8, rows).transpose(1, 0, 2), "h", "l")
    recip = lax.rsqrt(squares.transpose(1, 0, 2).reshape(2, group, 1) / e + EPS)
    q_recip, k_recip = recip[0], recip[1]
    query = turn(q_pre * q_recip * gq, cosine, sine, mine).astype(bf16)
    key = turn(k_pre * k_recip * gk, cosine, sine, mine).astype(bf16)
    keys = spread(key, "y", "x")
    values = spread(value, "x", "y").transpose(1, 0, 2, 3)
    kv = jnp.concatenate([keys, values], axis=-1)
    if outer > 1:
        kv = lax.all_gather(kv, "o", axis=0)
    kv = kv.reshape(-1, 2 * wide)
    attended, lse = attend(place, seq, kslot, query, kv, mine, HD, blk)
    proj = scatter8(jnp.dot(attended, w_o, preferred_element_type=f32), "h", "l")
    attn_branch, a_recip = norm_forward(proj, full_ga)
    mid = layer_input + attn_branch

    mg = gather8(mid.astype(bf16), "l", "y")
    gate_up = jnp.dot(mg, w_gu, preferred_element_type=f32)
    gate, up = gate_up[:, :units], gate_up[:, units:]
    sig = jax.nn.sigmoid(gate)
    silu = gate * sig
    hidden = (silu * up).astype(bf16)
    down = scatter8(jnp.dot(hidden, w_d, preferred_element_type=f32), "l", "y")
    mlp_branch, m_recip = norm_forward(down, full_gm)
    output = mid + mlp_branch
    d_down_f, local_gm = norm_backward(down, m_recip, full_gm, grad_output)
    dg = gather8(d_down_f.astype(bf16), "l", "y")
    d_hidden = lax.dot_general(dg, w_d, (((1,), (1,)), ((), ())), preferred_element_type=f32)
    d_gate = (d_hidden * up * sig * (1.0 + gate * (1.0 - sig))).astype(bf16)
    d_up = (d_hidden * silu).astype(bf16)
    d_gu = jnp.concatenate([d_gate, d_up], axis=1)
    d_mid = grad_output + scatter8(
        lax.dot_general(d_gu, w_gu, (((1,), (1,)), ((), ())), preferred_element_type=f32), "l", "y"
    )
    local_wd = lax.dot_general(hidden, dg, (((0,), (0,)), ((), ())), preferred_element_type=f32)
    local_wgu = lax.dot_general(mg, d_gu, (((0,), (0,)), ((), ())), preferred_element_type=f32)

    d_proj_f, local_ga = norm_backward(proj, a_recip, full_ga, d_mid)
    pg = gather8(d_proj_f.astype(bf16), "h", "l")
    d_att = lax.dot_general(pg, w_o, (((1,), (1,)), ((), ())), preferred_element_type=f32).astype(bf16)
    local_wo = lax.dot_general(attended, pg, (((0,), (0,)), ((), ())), preferred_element_type=f32)
    dq_rot, dkv = attend_back(place, seq, kslot, query, kv, attended, d_att, lse, mine, HD, blk)
    if outer > 1:
        dkv = lax.psum_scatter(
            dkv.reshape(outer, 2, 2, group, 2 * wide), "o", scatter_dimension=0, tiled=False
        )
    else:
        dkv = dkv.reshape(2, 2, group, 2 * wide)
    dk_rot = collect(dkv[..., :wide], "y", "x")
    d_value = collect(dkv[..., wide:].transpose(1, 0, 2, 3), "x", "y").astype(bf16)
    dq_n = turn(dq_rot, cosine, -sine, mine)
    dk_n = turn(dk_rot, cosine, -sine, mine)
    local_gq = jnp.sum(dq_n * q_pre * q_recip, axis=0)
    local_gk = jnp.sum(dk_n * k_pre * k_recip, axis=0)
    dq_s, dk_s = dq_n * gq, dk_n * gk
    sums = jnp.stack([jnp.sum(dq_s * q_pre, axis=-1), jnp.sum(dk_s * k_pre, axis=-1)])
    sums = sum8(sums.reshape(2, 8, rows).transpose(1, 0, 2), "h", "l").transpose(1, 0, 2)
    sums = sums.reshape(2, group, 1)
    d_qpre = (q_recip * dq_s - q_pre * (q_recip * q_recip * q_recip) * sums[0] / e).astype(bf16)
    d_kpre = (k_recip * dk_s - k_pre * (k_recip * k_recip * k_recip) * sums[1] / e).astype(bf16)
    d_qkv = jnp.concatenate([d_qpre, d_kpre, d_value], axis=1)
    grad_input = d_mid + scatter8(
        lax.dot_general(d_qkv, w_qkv, (((1,), (1,)), ((), ())), preferred_element_type=f32), "h", "l"
    )
    local_wqkv = lax.dot_general(xg, d_qkv, (((0,), (0,)), ((), ())), preferred_element_type=f32)

    ctx = ("o", "h", "l", "y", "c")

    def settle(local, a, b):
        cols = local.shape[1]
        part = halve(local.reshape(2, -1, cols), b)
        part = halve(part.reshape(2, -1, cols), a)
        if outer > 1:
            part = lax.psum_scatter(
                part.astype(bf16).reshape(outer, -1, cols), "o", scatter_dimension=0, tiled=False
            )
        return part.astype(bf16)

    half_d = d // 2
    got = lax.all_gather(settle(local_wqkv, "y", "x"), ctx, axis=0)
    got = got.reshape(outer, 2, 2, 2, 2, half_d // (2 * outer), 3 * wide)
    got = got.transpose(3, 0, 5, 1, 2, 4, 6).reshape(half_d, 8, 3, wide)

    def by_head(g):
        if aligned:
            g = g.reshape(half_d, 4, 2, 2, HD).transpose(0, 1, 3, 2, 4)
        return g.reshape(half_d, e).astype(f32)

    total_wq, total_wk, total_wv = by_head(got[:, :, 0]), by_head(got[:, :, 1]), by_head(got[:, :, 2])

    got = lax.all_gather(settle(local_wgu, "h", "x"), ctx, axis=0)
    got = got.reshape(outer, 2, 8, half_d // (2 * outer), 2, outer * 2, unit)
    got = got.transpose(4, 1, 0, 3, 5, 2, 6).reshape(2, half_d, f)
    total_wg, total_wu = got[0].astype(f32), got[1].astype(f32)

    got = lax.all_gather(settle(local_wd, "h", "x"), ctx, axis=0)
    half_u = units // 2
    if outer > 1:
        got = got.reshape(outer, 2, 8, half_u // (2 * outer), d).transpose(2, 1, 0, 3, 4)
        got = got.reshape(8, outer, unit, d).transpose(1, 0, 2, 3)
    else:
        got = got.reshape(2, 8, half_u // 2, d).transpose(1, 0, 2, 3)
    total_wd = got.reshape(f // 2, d).astype(f32)

    got = lax.all_gather(settle(local_wo, "y", "x"), every, axis=0)
    got = got.reshape(outer, 2, 2, 2, 2, 2, wide // (4 * outer), d)
    got = got.transpose(1, 2, 4, 5, 3, 0, 6, 7).reshape(4, 2, 2, wide // 2, d)
    if aligned:
        got = got.transpose(0, 2, 1, 3, 4)
    got = got.reshape(2, e // 2, d)
    total_wo = lax.dynamic_index_in_dim(got, index["x"], 0, keepdims=False).astype(f32)

    def own_part(local):
        zero = jnp.zeros((8, wide), f32)
        zero = lax.dynamic_update_slice_in_dim(zero, local.reshape(1, wide), team_a, 0)
        if aligned:
            zero = zero.reshape(4, 2, 2, HD).transpose(0, 2, 1, 3)
        return zero.reshape(-1)

    small = jnp.concatenate([own_part(local_gq), own_part(local_gk), local_ga, local_gm])
    small = lax.psum(small, every)

    def own_half(v):
        return lax.dynamic_index_in_dim(v.reshape(2, -1), index["x"], 0, keepdims=False)

    total_gq = own_half(small[:e])
    total_gk = own_half(small[e : 2 * e])
    total_ga = own_half(small[2 * e : 2 * e + d])
    total_gm = own_half(small[2 * e + d :])
    return (
        output,
        grad_input,
        total_wq,
        total_wk,
        total_wv,
        total_wo,
        total_wg,
        total_wu,
        total_wd,
        total_gq,
        total_gk,
        total_ga,
        total_gm,
    )


def solution(mesh):
    outer = mesh.shape["ctx"] // 16
    names = ("o", "h", "l", "y", "c", "x")
    fine = Mesh(mesh.devices.reshape(outer, 2, 2, 2, 2, 2), names)
    every, half = P(names), P("x")
    in_specs = (every, every, P()) + (every,) * 11
    out_specs = (every, every) + (half,) * 11
    return jax.shard_map(
        functools.partial(layer, outer=outer),
        mesh=fine,
        in_specs=in_specs,
        out_specs=out_specs,
        check_vma=False,
    )
```

```python
import functools
import math

import jax
import jax.numpy as jnp
from jax import lax
from jax.experimental import pallas as pl
from jax.experimental.pallas import tpu as pltpu
from jax.sharding import Mesh
from jax.sharding import PartitionSpec as P

NEG = -1e30


def dot(a, b, ca, cb):
    return lax.dot_general(a, b, (((ca,), (cb,)), ((), ())), preferred_element_type=jnp.float32)


def query_positions(seq_ref, tile, per, blk):
    lane = lax.broadcasted_iota(jnp.int32, (1, per * blk), 1)
    out = jnp.zeros((1, per * blk), jnp.int32)
    for b in range(per):
        first = seq_ref[tile * per + b] * blk
        out = jnp.where(lane // blk == b, first + lane - b * blk, out)
    return out


def sorted_load(src, dst, sem, count, blk, slot):
    def start(i, carry):
        pltpu.make_async_copy(
            src.at[pl.ds(pl.multiple_of(i * blk, blk), blk), :],
            dst.at[pl.ds(pl.multiple_of(slot(i) * blk, blk), blk), :],
            sem,
        ).start()
        return carry

    lax.fori_loop(0, count, start, 0)


def take(srcs, dst, sem, blk, slot):
    base = 0
    for src in srcs:
        sorted_load(src, dst, sem, src.shape[0] // blk, blk, lambda i, base=base: slot(base + i))
        base += src.shape[0] // blk


def finish(dst, sem):
    pltpu.make_async_copy(dst, dst, sem).wait()


def give(src, dsts, sem, blk, slot):
    base = 0
    for dst in dsts:

        def start(i, carry, dst=dst, base=base):
            pltpu.make_async_copy(
                src.at[pl.ds(pl.multiple_of(slot(base + i) * blk, blk), blk), :],
                dst.at[pl.ds(pl.multiple_of(i * blk, blk), blk), :],
                sem,
            ).start()
            return carry

        lax.fori_loop(0, dst.shape[0] // blk, start, 0)
        base += dst.shape[0] // blk


def attend_kernel(place_ref, seq_ref, kslot_ref, *refs, heads, head_size, blk, per, chunk, scale, pieces):
    q_ref, refs = refs[0], refs[1:]
    k_refs, v_refs, refs = refs[:pieces], refs[pieces : 2 * pieces], refs[2 * pieces :]
    o_ref, lse_ref, q_s, k_s, v_s, o_s, sems = refs
    nq = q_s.shape[0] // blk
    rows = per * blk
    take([q_ref], q_s, sems.at[0], blk, lambda i: place_ref[i])
    take(k_refs, k_s, sems.at[1], blk, lambda i: kslot_ref[i])
    take(v_refs, v_s, sems.at[2], blk, lambda i: kslot_ref[i])
    finish(q_s, sems.at[0])
    finish(k_s, sems.at[1])
    finish(v_s, sems.at[2])

    def tile_body(tile, carry):
        base = pl.multiple_of(tile * rows, rows)
        qpos = query_positions(seq_ref, tile, per, blk)
        full = (seq_ref[tile * per] * blk) // chunk
        last = ((seq_ref[tile * per + per - 1] + 1) * blk + chunk - 1) // chunk
        windows = [pl.ds(h * head_size, head_size) for h in range(heads)]
        qts = [q_s[pl.ds(base, rows), w] for w in windows]

        def step(j, states, masked):
            low = pl.multiple_of(j * chunk, chunk)
            krows = pl.ds(low, chunk)
            if masked:
                kpos = low + lax.broadcasted_iota(jnp.int32, (chunk, rows), 0)
                seen = kpos <= qpos
            scores = [dot(k_s[krows, w], qt, 1, 1) * scale for w, qt in zip(windows, qts)]
            out = []
            for w, s, (top, total, acc) in zip(windows, scores, states):
                if masked:
                    s = jnp.where(seen, s, NEG)
                top_new = jnp.maximum(top, jnp.max(s, axis=0, keepdims=True))
                p = jnp.exp(s - top_new)
                factor = jnp.exp(top - top_new)
                total = total * factor + jnp.sum(p, axis=0, keepdims=True)
                acc = acc * factor + dot(v_s[krows, w], p.astype(jnp.bfloat16), 0, 0)
                out.append((top_new, total, acc))
            return tuple(out)

        state = (
            jnp.full((1, rows), NEG, jnp.float32),
            jnp.zeros((1, rows), jnp.float32),
            jnp.zeros((head_size, rows), jnp.float32),
        )
        states = (state,) * heads
        states = lax.fori_loop(0, full, functools.partial(step, masked=False), states)
        states = lax.fori_loop(full, last, functools.partial(step, masked=True), states)
        for h, (top, total, acc) in enumerate(states):
            o_s[pl.ds(base, rows), windows[h]] = (acc / total).T.astype(o_s.dtype)
            lse_ref[pl.ds(tile * heads + h, 1), :] = top + jnp.log(total)
        return carry

    lax.fori_loop(0, nq // per, tile_body, 0)
    give(o_s, [o_ref], sems.at[0], blk, lambda i: place_ref[i])
    finish(o_s, sems.at[0])


ANY = pl.BlockSpec(memory_space=pl.ANY)
WHOLE = pl.BlockSpec(memory_space=pltpu.VMEM)


def attend(place, seq, kslot, q, ks, vs, heads, head_size, blk):
    nq = q.shape[0] // blk
    per = min(4, nq)
    rows = per * blk
    keys = sum(k.shape[0] for k in ks)
    return pl.pallas_call(
        functools.partial(
            attend_kernel, heads=heads, head_size=head_size, blk=blk, per=per, chunk=512,
            scale=1.0 / math.sqrt(head_size), pieces=len(ks),
        ),
        out_shape=(
            jax.ShapeDtypeStruct(q.shape, q.dtype),
            jax.ShapeDtypeStruct((nq // per * heads, rows), jnp.float32),
        ),
        grid_spec=pltpu.PrefetchScalarGridSpec(
            num_scalar_prefetch=3,
            grid=(),
            in_specs=[ANY] * (1 + 2 * len(ks)),
            out_specs=[ANY, WHOLE],
            scratch_shapes=[
                pltpu.VMEM(q.shape, q.dtype),
                pltpu.VMEM((keys, q.shape[1]), q.dtype),
                pltpu.VMEM((keys, q.shape[1]), q.dtype),
                pltpu.VMEM(q.shape, q.dtype),
                pltpu.SemaphoreType.DMA((3,)),
            ],
        ),
        compiler_params=pltpu.CompilerParams(vmem_limit_bytes=58 * 1024 * 1024),
        name="attend",
    )(place, seq, kslot, q, *ks, *vs)


def attend_back_kernel(
    place_ref, seq_ref, kslot_ref, *refs, heads, head_size, blk, per, chunk, scale, pieces
):
    (q_ref, o_ref, do_ref, lse_ref), refs = refs[:4], refs[4:]
    k_refs, v_refs, refs = refs[:pieces], refs[pieces : 2 * pieces], refs[2 * pieces :]
    dq_ref, refs = refs[0], refs[1:]
    dk_refs, dv_refs, refs = refs[:pieces], refs[pieces : 2 * pieces], refs[2 * pieces :]
    q_s, k_s, v_s, o_s, do_s, dq_s, dk_s, dv_s, sems = refs
    nq = q_s.shape[0] // blk
    rows = per * blk
    take([q_ref], q_s, sems.at[0], blk, lambda i: place_ref[i])
    take([o_ref], o_s, sems.at[1], blk, lambda i: place_ref[i])
    take([do_ref], do_s, sems.at[2], blk, lambda i: place_ref[i])
    take(k_refs, k_s, sems.at[3], blk, lambda i: kslot_ref[i])
    take(v_refs, v_s, sems.at[4], blk, lambda i: kslot_ref[i])
    dk_s[...] = jnp.zeros_like(dk_s)
    dv_s[...] = jnp.zeros_like(dv_s)
    finish(q_s, sems.at[0])
    finish(o_s, sems.at[1])
    finish(do_s, sems.at[2])
    finish(k_s, sems.at[3])
    finish(v_s, sems.at[4])

    def tile_body(tile, carry):
        base = pl.multiple_of(tile * rows, rows)
        qpos = query_positions(seq_ref, tile, per, blk)
        full = (seq_ref[tile * per] * blk) // chunk
        last = ((seq_ref[tile * per + per - 1] + 1) * blk + chunk - 1) // chunk
        windows = [pl.ds(h * head_size, head_size) for h in range(heads)]
        qts = [q_s[pl.ds(base, rows), w] for w in windows]
        dos = [do_s[pl.ds(base, rows), w] for w in windows]
        deltas, lses = [], []
        for h, w in enumerate(windows):
            prod = dos[h].astype(jnp.float32) * o_s[pl.ds(base, rows), w].astype(jnp.float32)
            deltas.append(jnp.sum(prod.T, axis=0, keepdims=True))
            lses.append(lse_ref[pl.ds(tile * heads + h, 1), :])

        def step(j, accs, masked):
            low = pl.multiple_of(j * chunk, chunk)
            krows = pl.ds(low, chunk)
            if masked:
                kpos = low + lax.broadcasted_iota(jnp.int32, (chunk, rows), 0)
                seen = kpos <= qpos
            out = []
            for h, w in enumerate(windows):
                kc = k_s[krows, w]
                s = dot(kc, qts[h], 1, 1) * scale - lses[h]
                if masked:
                    s = jnp.where(seen, s, NEG)
                p = jnp.exp(s)
                dp = dot(v_s[krows, w], dos[h], 1, 1)
                ds = (p * (dp - deltas[h])).astype(jnp.bfloat16)
                dv_s[krows, w] += dot(p.astype(jnp.bfloat16), dos[h], 1, 0)
                dk_s[krows, w] += dot(ds, qts[h], 1, 0)
                out.append(accs[h] + dot(kc, ds, 0, 0))
            return tuple(out)

        accs = (jnp.zeros((head_size, rows), jnp.float32),) * heads
        accs = lax.fori_loop(0, full, functools.partial(step, masked=False), accs)
        accs = lax.fori_loop(full, last, functools.partial(step, masked=True), accs)
        for h, w in enumerate(windows):
            dq_s[pl.ds(base, rows), w] = (accs[h] * scale).T
        return carry

    lax.fori_loop(0, nq // per, tile_body, 0)
    v_s[...] = dv_s[...].astype(v_s.dtype)
    give(v_s, dv_refs, sems.at[4], blk, lambda i: kslot_ref[i])
    k_s[...] = (dk_s[...] * scale).astype(k_s.dtype)
    give(k_s, dk_refs, sems.at[3], blk, lambda i: kslot_ref[i])
    give(dq_s, [dq_ref], sems.at[0], blk, lambda i: place_ref[i])
    finish(v_s, sems.at[4])
    finish(k_s, sems.at[3])
    finish(dq_s, sems.at[0])


def attend_back(place, seq, kslot, q, ks, vs, o, do, lse, heads, head_size, blk):
    nq = q.shape[0] // blk
    per = min(4, nq)
    keys = sum(k.shape[0] for k in ks)
    bf16, f32 = q.dtype, jnp.float32
    out = pl.pallas_call(
        functools.partial(
            attend_back_kernel, heads=heads, head_size=head_size, blk=blk, per=per, chunk=512,
            scale=1.0 / math.sqrt(head_size), pieces=len(ks),
        ),
        out_shape=(
            jax.ShapeDtypeStruct(q.shape, f32),
            *(jax.ShapeDtypeStruct(k.shape, bf16) for k in ks),
            *(jax.ShapeDtypeStruct(v.shape, bf16) for v in vs),
        ),
        grid_spec=pltpu.PrefetchScalarGridSpec(
            num_scalar_prefetch=3,
            grid=(),
            in_specs=[ANY] * 3 + [WHOLE] + [ANY] * (2 * len(ks)),
            out_specs=[ANY] * (1 + 2 * len(ks)),
            scratch_shapes=[
                pltpu.VMEM(q.shape, bf16),
                pltpu.VMEM((keys, q.shape[1]), bf16),
                pltpu.VMEM((keys, q.shape[1]), bf16),
                pltpu.VMEM(q.shape, bf16),
                pltpu.VMEM(q.shape, bf16),
                pltpu.VMEM(q.shape, f32),
                pltpu.VMEM((keys, q.shape[1]), f32),
                pltpu.VMEM((keys, q.shape[1]), f32),
                pltpu.SemaphoreType.DMA((5,)),
            ],
        ),
        compiler_params=pltpu.CompilerParams(vmem_limit_bytes=60 * 1024 * 1024),
        name="attend_back",
    )(place, seq, kslot, q, o, do, lse, *ks, *vs)
    return out[0], out[1 : 1 + len(ks)], out[1 + len(ks) :]


def rotate(x, cosine, sine, heads, head_size):
    parts = []
    for h in range(heads):
        part = x[:, h * head_size : (h + 1) * head_size]
        parts.append(part * cosine + pltpu.roll(part, head_size // 2, 1) * sine)
    return jnp.concatenate(parts, axis=1)


def prepare_kernel(pre_ref, recip_ref, gain_ref, cos_ref, sin_ref, q_ref, k_ref, *, heads, head_size):
    wide = heads * head_size
    for i, out in enumerate((q_ref, k_ref)):
        x = pre_ref[:, i * wide : (i + 1) * wide] * recip_ref[:, i : i + 1] * gain_ref[i : i + 1, :]
        out[...] = rotate(x, cos_ref[...], sin_ref[...], heads, head_size).astype(out.dtype)


def prepare(pre, recip, gain, cosine, sine, heads, head_size):
    rows, wide = pre.shape[0], heads * head_size
    step = 256
    return pl.pallas_call(
        functools.partial(prepare_kernel, heads=heads, head_size=head_size),
        out_shape=(jax.ShapeDtypeStruct((rows, wide), jnp.bfloat16),) * 2,
        grid=(rows // step,),
        in_specs=[
            pl.BlockSpec((step, 2 * wide), lambda i: (i, 0)),
            pl.BlockSpec((step, 2), lambda i: (i, 0)),
            pl.BlockSpec((2, wide), lambda i: (0, 0)),
            pl.BlockSpec((step, head_size), lambda i: (i, 0)),
            pl.BlockSpec((step, head_size), lambda i: (i, 0)),
        ],
        out_specs=[pl.BlockSpec((step, wide), lambda i: (i, 0))] * 2,
        name="prepare",
    )(pre, recip, gain, cosine, sine)


def unturn_kernel(
    dq_ref, dka_ref, dkb_ref, pre_ref, recip_ref, gain_ref, cos_ref, sin_ref,
    ds_ref, sum_ref, gg_ref, *, heads, head_size
):
    wide = heads * head_size
    dk = dka_ref[...] + dkb_ref[...].astype(jnp.float32)

    @pl.when(pl.program_id(0) == 0)
    def _():
        gg_ref[...] = jnp.zeros_like(gg_ref)

    for i, d in enumerate((dq_ref[...], dk)):
        cols = slice(i * wide, (i + 1) * wide)
        n = rotate(d, cos_ref[...], -sin_ref[...], heads, head_size)
        pre = pre_ref[:, cols]
        gg_ref[i : i + 1, :] += jnp.sum(n * pre * recip_ref[:, i : i + 1], axis=0, keepdims=True)
        scaled = n * gain_ref[i : i + 1, :]
        ds_ref[:, cols] = scaled
        sum_ref[i : i + 1, :] = jnp.sum((scaled * pre).T, axis=0, keepdims=True)


def unturn(dq, dka, dkb, pre, recip, gain, cosine, sine, heads, head_size):
    rows, wide = pre.shape[0], heads * head_size
    step = 256
    by_row = lambda n: pl.BlockSpec((step, n), lambda i: (i, 0))
    fixed = pl.BlockSpec((2, wide), lambda i: (0, 0))
    return pl.pallas_call(
        functools.partial(unturn_kernel, heads=heads, head_size=head_size),
        out_shape=(
            jax.ShapeDtypeStruct((rows, 2 * wide), jnp.float32),
            jax.ShapeDtypeStruct((2, rows), jnp.float32),
            jax.ShapeDtypeStruct((2, wide), jnp.float32),
        ),
        grid=(rows // step,),
        in_specs=[
            by_row(wide), by_row(wide), by_row(wide), by_row(2 * wide), by_row(2), fixed,
            by_row(head_size), by_row(head_size),
        ],
        out_specs=[by_row(2 * wide), pl.BlockSpec((2, step), lambda i: (0, i)), fixed],
        name="unturn",
    )(dq, dka, dkb, pre, recip, gain, cosine, sine)


def unpack_kernel(src_ref, *refs, plan, pieces, cover):
    outs = refs[: len(plan[0])]
    got, wide, in_sems, out_sems = refs[len(outs) :]

    def fetch(p):
        return pltpu.make_async_copy(src_ref.at[p], got.at[p % 2], in_sems.at[p % 2])

    def parts(p):
        copies = []
        for out, moves in zip(outs, plan[p]):
            for rows, cols, drow, dcol in moves:
                copies.append(
                    pltpu.make_async_copy(
                        wide.at[p % 2, pl.ds(*rows), pl.ds(*cols)],
                        out.at[pl.ds(drow, rows[1]), pl.ds(dcol, cols[1])],
                        out_sems.at[p % 2],
                    )
                )
        return copies

    def done(p):
        window = wide.at[p % 2, pl.ds(0, cover), :]
        pltpu.make_async_copy(window, window, out_sems.at[p % 2]).wait()

    fetch(0).start()
    for p in range(pieces):
        if p + 1 < pieces:
            fetch(p + 1).start()
        fetch(p).wait()
        if p >= 2:
            done(p - 2)
        wide[p % 2] = got[p % 2].astype(jnp.float32)
        for copy in parts(p):
            copy.start()
    for p in range(max(pieces - 2, 0), pieces):
        done(p)


def unpack(src, shapes, plan, cover):
    pieces, rows, cols = src.shape
    return pl.pallas_call(
        functools.partial(unpack_kernel, plan=plan, pieces=pieces, cover=cover),
        out_shape=tuple(jax.ShapeDtypeStruct(s, jnp.float32) for s in shapes),
        in_specs=[ANY],
        out_specs=[ANY] * len(shapes),
        scratch_shapes=[
            pltpu.VMEM((2, rows, cols), src.dtype),
            pltpu.VMEM((2, rows, cols), jnp.float32),
            pltpu.SemaphoreType.DMA((2,)),
            pltpu.SemaphoreType.DMA((2,)),
        ],
        compiler_params=pltpu.CompilerParams(vmem_limit_bytes=40 * 1024 * 1024),
        name="unpack",
    )(src)


EPS = 1e-06
THETA = 500000.0
HD = 128


def norm_forward(value, gain):
    recip = lax.rsqrt(jnp.mean(value * value, axis=-1, keepdims=True) + EPS)
    return (value * recip * gain, recip)


def norm_backward(value, recip, gain, grad_out):
    scaled = grad_out * gain
    width = value.shape[-1]
    grad_in = (
        recip * scaled
        - value * (recip * recip * recip) * jnp.sum(scaled * value, axis=-1, keepdims=True) / width
    )
    grad_gain = jnp.sum(grad_out * value * recip, axis=0)
    return (grad_in, grad_gain)


def flip(value, *axes):
    last = 2 ** len(axes) - 1
    return lax.ppermute(value, axes, [(i, i ^ last) for i in range(last + 1)])


def gather8(x, a, b):
    mine = jnp.stack([x, flip(x, b), flip(x, a), flip(x, a, b)])
    other = flip(mine, "c")
    return jnp.concatenate([mine, other]).reshape(8 * x.shape[0], x.shape[1])


def scatter8(x, a, b):
    bf16 = jnp.bfloat16
    parts = x.astype(bf16).reshape(2, 4, x.shape[0] // 8, x.shape[1])
    mine = x.reshape(parts.shape)[0] + flip(parts[1], "c").astype(jnp.float32)
    out = mine.astype(bf16)
    return (
        mine[0]
        + flip(out[1], b).astype(jnp.float32)
        + flip(out[2], a).astype(jnp.float32)
        + flip(out[3], a, b).astype(jnp.float32)
    )


def sum8(x, a, b):
    t = x.reshape((2, 2, 2) + x.shape[1:])
    for axis, name in enumerate(("c", a, b)):
        t = t + jnp.flip(flip(t, name), axis)
    return t.reshape(x.shape)


def in_order(value, axis, name):
    return jnp.where(lax.axis_index(name) == 1, jnp.flip(value, axis), value)


def gather4(x, a, b):
    pair = jnp.stack([x, flip(x, a)])
    quad = jnp.stack([pair, flip(pair, b)])
    return in_order(in_order(quad, 1, a), 0, b)


def halve(x, name):
    me = lax.axis_index(name)
    keep = lax.dynamic_index_in_dim(x, me, 0, keepdims=False)
    send = lax.dynamic_index_in_dim(x, 1 - me, 0, keepdims=False)
    return keep.astype(jnp.float32) + flip(send.astype(jnp.bfloat16), name).astype(jnp.float32)


def layer(
    layer_input,
    grad_output,
    positions,
    w_query,
    w_key,
    w_value,
    w_out,
    w_gate,
    w_up,
    w_down,
    gain_query,
    gain_key,
    gain_attn,
    gain_mlp,
    *,
    outer,
):
    f32 = jnp.float32
    bf16 = jnp.bfloat16
    rows, d = layer_input.shape
    drows, e = w_query.shape
    f = w_gate.shape[1]
    blk = rows // 2
    devices = positions.shape[0] // rows
    teams = devices // 8
    every = ("o", "h", "l", "y", "c", "x")
    heads = e // HD
    mine = heads // 8
    wide = mine * HD
    index = {name: lax.axis_index(name) for name in every}

    def by_team(w):
        return w.reshape(drows, mine, 8, HD).transpose(2, 0, 1, 3).reshape(8, drows, wide)

    gains = jnp.concatenate([gain_query, gain_key, gain_attn, gain_mlp])
    pad = drows * 128 - gains.shape[0]
    gains = jnp.pad(gains, (0, pad)).reshape(1, drows, 128)
    payload = jnp.concatenate(
        [by_team(w_query), by_team(w_key), by_team(w_value), jnp.broadcast_to(gains, (8, drows, 128))],
        axis=2,
    )
    payload = lax.all_to_all(payload, ("h", "l", "c"), 0, 0, tiled=True)
    payload = gather4(payload, "y", "x")
    if outer > 1:
        payload = lax.all_gather(payload, "o", axis=0)
    else:
        payload = payload[None]
    payload = payload.reshape(outer, 2, 2, 2, 2, 2, drows, 3 * wide + 128)
    payload = payload.transpose(0, 3, 4, 2, 5, 1, 6, 7).reshape(d, 3 * wide + 128)
    w_qkv = payload[:, : 3 * wide]
    gains = payload[:, 3 * wide :].reshape(devices, drows * 128)
    e_own, d_own = e // devices, d // devices
    full_gq = gains[:, :e_own].reshape(e)
    full_gk = gains[:, e_own : 2 * e_own].reshape(e)
    full_ga = gains[:, 2 * e_own : 2 * e_own + d_own].reshape(1, d).astype(f32)
    full_gm = gains[:, 2 * e_own + d_own : 2 * e_own + 2 * d_own].reshape(1, d).astype(f32)
    team_a = index["h"] * 4 + index["l"] * 2 + index["c"]

    def own_gain(g):
        return lax.dynamic_index_in_dim(g.reshape(mine, 8, HD), team_a, 1, keepdims=False).reshape(wide)

    gain_qk = jnp.stack([own_gain(full_gq), own_gain(full_gk)]).astype(f32)

    if outer == 1:
        w_o = gather4(w_out, "h", "x").transpose(1, 0, 2, 3).reshape(wide, d)
        w_o = lax.ppermute(
            w_o, ("h", "l", "y"), [(i, 2 * (i % 4) + i // 4) for i in range(8)]
        )
    else:
        w_o = lax.all_gather(w_out, every, axis=0, tiled=True).reshape(mine, 8, HD, d)
        w_o = lax.dynamic_index_in_dim(w_o, team_a, 1, keepdims=False).reshape(wide, d)

    unit = f // (8 * outer * 2)
    units = outer * 2 * unit

    def by_unit(w):
        return w.reshape(drows, outer * 2, 8, unit).transpose(2, 0, 1, 3).reshape(8, drows, units)

    ff = jnp.concatenate([by_unit(w_gate), by_unit(w_up)], axis=2)
    ff = lax.all_to_all(ff, ("l", "y", "c"), 0, 0, tiled=True)
    ff = gather4(ff, "h", "x")
    w_d = gather4(w_down, "h", "x")
    if outer > 1:
        ff = lax.all_gather(ff, "o", axis=0)
        w_d = lax.all_gather(w_d, "o", axis=0)
    else:
        ff, w_d = ff[None], w_d[None]
    ff = ff.reshape(outer, 2, 2, 2, 2, 2, drows, 2 * units)
    w_gu = ff.transpose(0, 2, 3, 4, 5, 1, 6, 7).reshape(d, 2 * units)
    w_d = w_d.transpose(0, 2, 1, 3, 4).reshape(units, d)

    table = positions.reshape(outer, 2, 2, 2, 2, 2, rows)[..., ::blk] // blk
    for axis, name in enumerate(every):
        if name != "o":
            table = in_order(table, axis, name)
    kslot = table.transpose(0, 5, 3, 4, 1, 2, 6)
    qblocks = lax.dynamic_index_in_dim(kslot, index["o"], 0, keepdims=False)[0, 0].reshape(-1)
    kslot = kslot.reshape(-1)
    nq = qblocks.shape[0]
    place = jnp.sum((qblocks[None, :] < qblocks[:, None]).astype(jnp.int32), axis=1)
    seq = jnp.sum(
        jnp.where(place[None, :] == jnp.arange(nq)[:, None], qblocks[None, :], 0), axis=1
    ).astype(jnp.int32)
    group_pos = (qblocks[:, None] * blk + jnp.arange(blk, dtype=jnp.int32)[None, :]).reshape(-1)
    freqs = THETA ** (-(2.0 * jnp.arange(HD // 2, dtype=f32)) / HD)
    angles = group_pos.astype(f32)[:, None] * freqs[None, :]
    cosine, sine = jnp.cos(angles), jnp.sin(angles)
    cosine = jnp.concatenate([cosine, cosine], axis=1)
    sine = jnp.concatenate([-sine, sine], axis=1)

    xg = gather8(layer_input.astype(bf16), "h", "l")
    group = xg.shape[0]
    pre = jnp.dot(xg, w_qkv, preferred_element_type=f32)
    pre_qk, value = pre[:, : 2 * wide], pre[:, 2 * wide :].astype(bf16)
    squares = jnp.sum((pre_qk * pre_qk).reshape(group, 2, wide), axis=-1).T
    squares = sum8(squares.reshape(2, 8, rows).transpose(1, 0, 2), "h", "l")
    recip = lax.rsqrt(squares.transpose(1, 0, 2).reshape(2, group) / e + EPS).T
    query, key = prepare(pre_qk, recip, gain_qk, cosine, sine, mine, HD)
    key_y, value_x = flip(key, "y"), flip(value, "x")
    keys = [key, key_y, flip(key, "x"), flip(key_y, "x")]
    values = [value, flip(value, "y"), value_x, flip(value_x, "y")]
    if outer > 1:
        keys = [lax.all_gather(jnp.stack(keys), "o", axis=0).reshape(-1, wide)]
        values = [lax.all_gather(jnp.stack(values), "o", axis=0).reshape(-1, wide)]
    attended, lse = attend(place, seq, kslot, query, keys, values, mine, HD, blk)
    proj = scatter8(jnp.dot(attended, w_o, preferred_element_type=f32), "h", "l")
    attn_branch, a_recip = norm_forward(proj, full_ga)
    mid = layer_input + attn_branch

    mg = gather8(mid.astype(bf16), "l", "y")
    gate_up = jnp.dot(mg, w_gu, preferred_element_type=f32)
    gate, up = gate_up[:, :units], gate_up[:, units:]
    sig = jax.nn.sigmoid(gate)
    silu = gate * sig
    hidden = (silu * up).astype(bf16)
    down = scatter8(jnp.dot(hidden, w_d, preferred_element_type=f32), "l", "y")
    mlp_branch, m_recip = norm_forward(down, full_gm)
    output = mid + mlp_branch
    d_down_f, local_gm = norm_backward(down, m_recip, full_gm, grad_output)
    dg = gather8(d_down_f.astype(bf16), "l", "y")
    d_hidden = lax.dot_general(dg, w_d, (((1,), (1,)), ((), ())), preferred_element_type=f32)
    d_gate = (d_hidden * up * sig * (1.0 + gate * (1.0 - sig))).astype(bf16)
    d_up = (d_hidden * silu).astype(bf16)
    d_gu = jnp.concatenate([d_gate, d_up], axis=1)
    d_mid = grad_output + scatter8(
        lax.dot_general(d_gu, w_gu, (((1,), (1,)), ((), ())), preferred_element_type=f32), "l", "y"
    )
    local_wd = lax.dot_general(hidden, dg, (((0,), (0,)), ((), ())), preferred_element_type=f32)
    local_wgu = lax.dot_general(mg, d_gu, (((0,), (0,)), ((), ())), preferred_element_type=f32)

    d_proj_f, local_ga = norm_backward(proj, a_recip, full_ga, d_mid)
    pg = gather8(d_proj_f.astype(bf16), "h", "l")
    d_att = lax.dot_general(pg, w_o, (((1,), (1,)), ((), ())), preferred_element_type=f32).astype(bf16)
    local_wo = lax.dot_general(attended, pg, (((0,), (0,)), ((), ())), preferred_element_type=f32)
    dq_rot, dk, dv = attend_back(
        place, seq, kslot, query, keys, values, attended, d_att, lse, mine, HD, blk
    )
    if outer > 1:
        def own_quarter(g):
            g = g[0].reshape(outer, 4, group, wide)
            return list(lax.psum_scatter(g, "o", scatter_dimension=0, tiled=False))

        dk, dv = own_quarter(dk), own_quarter(dv)
    dk_a = dk[0].astype(f32) + flip(dk[2], "x").astype(f32)
    dk_b = flip((dk[1].astype(f32) + flip(dk[3], "x").astype(f32)).astype(bf16), "y")
    dv_a = dv[0].astype(f32) + flip(dv[1], "y").astype(f32)
    dv_b = flip((dv[2].astype(f32) + flip(dv[3], "y").astype(f32)).astype(bf16), "x")
    d_value = (dv_a + dv_b.astype(f32)).astype(bf16)
    d_scaled, sums, local_gqk = unturn(
        dq_rot, dk_a, dk_b, pre_qk, recip, gain_qk, cosine, sine, mine, HD
    )
    sums = sum8(sums.reshape(2, 8, rows).transpose(1, 0, 2), "h", "l").transpose(1, 0, 2)
    sums = sums.reshape(2, group).T
    cubes = recip * recip * recip * sums / e
    d_qk = (
        recip[:, :, None] * d_scaled.reshape(group, 2, wide)
        - pre_qk.reshape(group, 2, wide) * cubes[:, :, None]
    ).astype(bf16)
    d_qkv = jnp.concatenate([d_qk.reshape(group, 2 * wide), d_value], axis=1)
    grad_input = d_mid + scatter8(
        lax.dot_general(d_qkv, w_qkv, (((1,), (1,)), ((), ())), preferred_element_type=f32), "h", "l"
    )
    local_wqkv = lax.dot_general(xg, d_qkv, (((0,), (0,)), ((), ())), preferred_element_type=f32)

    ctx = ("o", "h", "l", "y", "c")

    def settle(local, a, b):
        cols = local.shape[1]
        part = halve(local.reshape(2, -1, cols), b)
        part = halve(part.reshape(2, -1, cols), a)
        if outer > 1:
            part = lax.psum_scatter(
                part.astype(bf16).reshape(outer, -1, cols), "o", scatter_dimension=0, tiled=False
            )
        return part.astype(bf16)

    half_d, half_f = d // 2, f // 2
    part_gu, part_d, part_o = settle(local_wgu, "h", "x"), settle(local_wd, "h", "x"), settle(local_wo, "y", "x")
    part_qkv = settle(local_wqkv, "y", "x")
    n_qk, n_am = wide, d
    lines = -(-max(n_qk, n_am) // (3 * wide))
    lines = -(-lines // 16) * 16

    def line(v, n):
        return jnp.pad(v.reshape(2, n), ((0, 0), (0, lines * 3 * wide - n)))

    small = jnp.stack(
        [
            line(local_gqk.reshape(2, 2, -1).transpose(1, 0, 2), n_qk),
            line(jnp.stack([local_ga, local_gm]).reshape(2, 2, -1).transpose(1, 0, 2), n_am),
        ],
        axis=1,
    )
    small = halve(small, "x")
    small = halve(small, "y")
    if outer > 1:
        small = lax.psum(small, "o") / outer
    small = small.reshape(lines, 3 * wide).astype(bf16)
    part_qkv = jnp.concatenate([part_qkv, small])
    n_gu, n_d, n_o, n_qkv = part_gu.shape[0], part_d.shape[0], part_o.shape[0], part_qkv.shape[0] - lines

    if outer == 1:
        first = lax.all_gather(jnp.concatenate([part_gu, part_d, part_o]), ctx, axis=0).reshape(16, -1, d)
        last = lax.all_gather(part_qkv, ctx, axis=0).reshape(16, -1, 3 * wide)
        plan_first, plan_last = [], []
        for p in range(16):
            h, l, y, c = p >> 3, (p >> 2) & 1, (p >> 1) & 1, p & 1
            team_f, team_q = 4 * l + 2 * y + c, 4 * h + 2 * l + c
            ups = [
                [
                    ((0, n_gu), (m * units + o * unit, unit), h * n_gu, (o * 8 + team_f) * unit)
                    for o in range(2)
                ]
                for m in range(2)
            ]
            downs = [((n_gu, n_d), (0, d), team_f * unit + h * n_d, 0)]
            os = [((n_gu + n_d, n_o), (0, d), team_q * HD + y * n_o, 0)]
            plan_first.append([*ups, downs, os])
            plan_last.append(
                [
                    [
                        ((0, n_qkv), (m * wide + o * HD, HD), y * n_qkv, (o * 8 + team_q) * HD)
                        for o in range(mine)
                    ]
                    for m in range(3)
                ]
            )
        total_wg, total_wu, total_wd, total_wo = unpack(
            first, [(half_d, f), (half_d, f), (half_f, d), (e // 2, d)], plan_first, n_gu + n_d + n_o
        )
        total_wq, total_wk, total_wv = unpack(last, [(half_d, e)] * 3, plan_last, n_qkv)
        got_small = last[:, n_qkv:]
    else:
        got = lax.all_gather(part_qkv, ctx, axis=0)
        got_small = got.reshape(-1, n_qkv + lines, 3 * wide)[:, n_qkv:]
        got = got.reshape(outer, 2, 2, 2, 2, n_qkv + lines, 3 * wide)[..., :n_qkv, :]
        got = got.transpose(3, 0, 5, 1, 2, 4, 6).reshape(half_d, 8, 3, mine, HD)
        got = got.transpose(2, 0, 3, 1, 4).reshape(3, half_d, e)
        total_wq, total_wk, total_wv = got[0].astype(f32), got[1].astype(f32), got[2].astype(f32)
        got = lax.all_gather(part_gu, ctx, axis=0)
        got = got.reshape(outer, 2, 8, n_gu, 2, outer * 2, unit)
        got = got.transpose(4, 1, 0, 3, 5, 2, 6).reshape(2, half_d, f)
        total_wg, total_wu = got[0].astype(f32), got[1].astype(f32)
        got = lax.all_gather(part_d, ctx, axis=0)
        got = got.reshape(outer, 2, 8, n_d, d).transpose(2, 1, 0, 3, 4)
        total_wd = got.reshape(8, outer, unit, d).transpose(1, 0, 2, 3).reshape(half_f, d).astype(f32)
        got = lax.all_gather(part_o, ctx, axis=0)
        got = got.reshape(outer, 2, 2, 2, 2, n_o, d).transpose(1, 2, 4, 3, 0, 5, 6)
        total_wo = got.reshape(e // 2, d).astype(f32)

    got_small = got_small.astype(f32).reshape(outer, 4, 2, 2, lines * 3 * wide)
    if outer > 1:
        got_small = jnp.sum(got_small, axis=0)
    else:
        got_small = got_small[0]
    qk = got_small[:, 0, :, :n_qk].reshape(8, 2, mine // 2, HD).transpose(1, 2, 0, 3).reshape(2, e // 2)
    total_gq, total_gk = qk[0], qk[1]
    am = jnp.sum(got_small[:, 1, :, :n_am], axis=(0, 1)).reshape(2, half_d)
    total_ga, total_gm = am[0], am[1]
    return (
        output,
        grad_input,
        total_wq,
        total_wk,
        total_wv,
        total_wo,
        total_wg,
        total_wu,
        total_wd,
        total_gq,
        total_gk,
        total_ga,
        total_gm,
    )


def solution(mesh):
    outer = mesh.shape["ctx"] // 16
    names = ("o", "h", "l", "y", "c", "x")
    fine = Mesh(mesh.devices.reshape(outer, 2, 2, 2, 2, 2), names)
    every, half = P(names), P("x")
    in_specs = (every, every, P()) + (every,) * 11
    out_specs = (every, every) + (half,) * 11
    return jax.shard_map(
        functools.partial(layer, outer=outer),
        mesh=fine,
        in_specs=in_specs,
        out_specs=out_specs,
        check_vma=False,
    )
```

```python
import functools
import math

import jax
import jax.numpy as jnp
from jax import lax
from jax.experimental import pallas as pl
from jax.experimental.pallas import tpu as pltpu
from jax.sharding import Mesh
from jax.sharding import PartitionSpec as P

EPS = 1e-06
NEG = -1e30


def dot(a, b, ca, cb):
    return lax.dot_general(a, b, (((ca,), (cb,)), ((), ())), preferred_element_type=jnp.float32)


def query_positions(seq_ref, tile, per, blk):
    lane = lax.broadcasted_iota(jnp.int32, (1, per * blk), 1)
    out = jnp.zeros((1, per * blk), jnp.int32)
    for b in range(per):
        first = seq_ref[tile * per + b] * blk
        out = jnp.where(lane // blk == b, first + lane - b * blk, out)
    return out


def sorted_load(src, dst, sem, count, blk, slot):
    def start(i, carry):
        pltpu.make_async_copy(
            src.at[pl.ds(pl.multiple_of(i * blk, blk), blk), :],
            dst.at[pl.ds(pl.multiple_of(slot(i) * blk, blk), blk), :],
            sem,
        ).start()
        return carry

    lax.fori_loop(0, count, start, 0)


def take(srcs, dst, sem, blk, slot):
    base = 0
    for src in srcs:
        sorted_load(src, dst, sem, src.shape[0] // blk, blk, lambda i, base=base: slot(base + i))
        base += src.shape[0] // blk


def finish(dst, sem):
    pltpu.make_async_copy(dst, dst, sem).wait()


def give(src, dsts, sem, blk, slot):
    base = 0
    for dst in dsts:

        def start(i, carry, dst=dst, base=base):
            pltpu.make_async_copy(
                src.at[pl.ds(pl.multiple_of(slot(base + i) * blk, blk), blk), :],
                dst.at[pl.ds(pl.multiple_of(i * blk, blk), blk), :],
                sem,
            ).start()
            return carry

        lax.fori_loop(0, dst.shape[0] // blk, start, 0)
        base += dst.shape[0] // blk


def attend_kernel(place_ref, seq_ref, kslot_ref, *refs, heads, head_size, blk, per, chunk, scale, pieces):
    (q_ref, wo_ref), refs = refs[:2], refs[2:]
    k_refs, v_refs, refs = refs[:pieces], refs[pieces : 2 * pieces], refs[2 * pieces :]
    o_ref, lse_ref, mine_ref, send_ref, q_s, k_s, v_s, o_s, wo_s, part_s, low_s, sems = refs
    nq = q_s.shape[0] // blk
    rows = per * blk
    take([q_ref], q_s, sems.at[0], blk, lambda i: place_ref[i])
    take(k_refs, k_s, sems.at[1], blk, lambda i: kslot_ref[i])
    take(v_refs, v_s, sems.at[2], blk, lambda i: kslot_ref[i])
    pltpu.make_async_copy(wo_ref, wo_s, sems.at[3]).start()
    finish(q_s, sems.at[0])
    finish(k_s, sems.at[1])
    finish(v_s, sems.at[2])
    finish(wo_s, sems.at[3])

    def tile_body(tile, carry):
        base = pl.multiple_of(tile * rows, rows)
        qpos = query_positions(seq_ref, tile, per, blk)
        full = (seq_ref[tile * per] * blk) // chunk
        last = ((seq_ref[tile * per + per - 1] + 1) * blk + chunk - 1) // chunk
        windows = [pl.ds(h * head_size, head_size) for h in range(heads)]
        qts = [q_s[pl.ds(base, rows), w] for w in windows]

        def step(j, states, masked):
            low = pl.multiple_of(j * chunk, chunk)
            krows = pl.ds(low, chunk)
            if masked:
                kpos = low + lax.broadcasted_iota(jnp.int32, (chunk, rows), 0)
                seen = kpos <= qpos
            scores = [dot(k_s[krows, w], qt, 1, 1) * scale for w, qt in zip(windows, qts)]
            out = []
            for w, s, (top, total, acc) in zip(windows, scores, states):
                if masked:
                    s = jnp.where(seen, s, NEG)
                top_new = jnp.maximum(top, jnp.max(s, axis=0, keepdims=True))
                p = jnp.exp(s - top_new)
                factor = jnp.exp(top - top_new)
                total = total * factor + jnp.sum(p, axis=0, keepdims=True)
                acc = acc * factor + dot(v_s[krows, w], p.astype(jnp.bfloat16), 0, 0)
                out.append((top_new, total, acc))
            return tuple(out)

        state = (
            jnp.full((1, rows), NEG, jnp.float32),
            jnp.zeros((1, rows), jnp.float32),
            jnp.zeros((head_size, rows), jnp.float32),
        )
        states = (state,) * heads
        states = lax.fori_loop(0, full, functools.partial(step, masked=False), states)
        states = lax.fori_loop(full, last, functools.partial(step, masked=True), states)
        for h, (top, total, acc) in enumerate(states):
            o_s[pl.ds(base, rows), windows[h]] = (acc / total).T.astype(o_s.dtype)
            lse_ref[pl.ds(tile * heads + h, 1), :] = top + jnp.log(total)
        part = dot(o_s[pl.ds(base, rows), :], wo_s[...], 1, 0)
        part_s[pl.ds(base, rows), :] = part
        low_s[pl.ds(base, rows), :] = part.astype(low_s.dtype)
        return carry

    lax.fori_loop(0, nq // per, tile_body, 0)
    half = nq // 2
    give(part_s, [mine_ref], sems.at[1], blk, lambda i: place_ref[i])
    give(low_s, [send_ref], sems.at[2], blk, lambda i: place_ref[half + i])
    give(o_s, [o_ref], sems.at[0], blk, lambda i: place_ref[i])
    finish(mine_ref, sems.at[1])
    finish(send_ref, sems.at[2])
    finish(o_s, sems.at[0])


ANY = pl.BlockSpec(memory_space=pl.ANY)
WHOLE = pl.BlockSpec(memory_space=pltpu.VMEM)


def attend(place, seq, kslot, q, ks, vs, w_o, heads, head_size, blk):
    nq = q.shape[0] // blk
    per = min(4, nq)
    rows = per * blk
    keys = sum(k.shape[0] for k in ks)
    return pl.pallas_call(
        functools.partial(
            attend_kernel, heads=heads, head_size=head_size, blk=blk, per=per, chunk=512,
            scale=1.0 / math.sqrt(head_size), pieces=len(ks),
        ),
        out_shape=(
            jax.ShapeDtypeStruct(q.shape, q.dtype),
            jax.ShapeDtypeStruct((nq // per * heads, rows), jnp.float32),
            jax.ShapeDtypeStruct((q.shape[0] // 2, w_o.shape[1]), jnp.float32),
            jax.ShapeDtypeStruct((q.shape[0] // 2, w_o.shape[1]), q.dtype),
        ),
        grid_spec=pltpu.PrefetchScalarGridSpec(
            num_scalar_prefetch=3,
            grid=(),
            in_specs=[ANY] * (2 + 2 * len(ks)),
            out_specs=[ANY, WHOLE, ANY, ANY],
            scratch_shapes=[
                pltpu.VMEM(q.shape, q.dtype),
                pltpu.VMEM((keys, q.shape[1]), q.dtype),
                pltpu.VMEM((keys, q.shape[1]), q.dtype),
                pltpu.VMEM(q.shape, q.dtype),
                pltpu.VMEM(w_o.shape, q.dtype),
                pltpu.VMEM((q.shape[0], w_o.shape[1]), jnp.float32),
                pltpu.VMEM((q.shape[0], w_o.shape[1]), q.dtype),
                pltpu.SemaphoreType.DMA((4,)),
            ],
        ),
        compiler_params=pltpu.CompilerParams(vmem_limit_bytes=58 * 1024 * 1024),
        name="attend",
    )(place, seq, kslot, q, w_o, *ks, *vs)


def attend_back_kernel(
    place_ref, seq_ref, kslot_ref, *refs, heads, head_size, blk, per, chunk, scale, pieces
):
    (q_ref, o_ref, do_ref, lse_ref), refs = refs[:4], refs[4:]
    k_refs, v_refs, refs = refs[:pieces], refs[pieces : 2 * pieces], refs[2 * pieces :]
    dq_ref, refs = refs[0], refs[1:]
    dk_refs, dv_refs, refs = refs[:pieces], refs[pieces : 2 * pieces], refs[2 * pieces :]
    q_s, k_s, v_s, o_s, do_s, dq_s, dk_s, dv_s, sems = refs
    nq = q_s.shape[0] // blk
    rows = per * blk
    take([q_ref], q_s, sems.at[0], blk, lambda i: place_ref[i])
    take([o_ref], o_s, sems.at[1], blk, lambda i: place_ref[i])
    take([do_ref], do_s, sems.at[2], blk, lambda i: place_ref[i])
    take(k_refs, k_s, sems.at[3], blk, lambda i: kslot_ref[i])
    take(v_refs, v_s, sems.at[4], blk, lambda i: kslot_ref[i])
    dk_s[...] = jnp.zeros_like(dk_s)
    dv_s[...] = jnp.zeros_like(dv_s)
    finish(q_s, sems.at[0])
    finish(o_s, sems.at[1])
    finish(do_s, sems.at[2])
    finish(k_s, sems.at[3])
    finish(v_s, sems.at[4])

    def tile_body(tile, carry):
        base = pl.multiple_of(tile * rows, rows)
        qpos = query_positions(seq_ref, tile, per, blk)
        full = (seq_ref[tile * per] * blk) // chunk
        last = ((seq_ref[tile * per + per - 1] + 1) * blk + chunk - 1) // chunk
        windows = [pl.ds(h * head_size, head_size) for h in range(heads)]
        qts = [q_s[pl.ds(base, rows), w] for w in windows]
        dos = [do_s[pl.ds(base, rows), w] for w in windows]
        deltas, lses = [], []
        for h, w in enumerate(windows):
            prod = dos[h].astype(jnp.float32) * o_s[pl.ds(base, rows), w].astype(jnp.float32)
            deltas.append(jnp.sum(prod.T, axis=0, keepdims=True))
            lses.append(lse_ref[pl.ds(tile * heads + h, 1), :])

        def step(j, accs, masked):
            low = pl.multiple_of(j * chunk, chunk)
            krows = pl.ds(low, chunk)
            if masked:
                kpos = low + lax.broadcasted_iota(jnp.int32, (chunk, rows), 0)
                seen = kpos <= qpos
            out = []
            for h, w in enumerate(windows):
                kc = k_s[krows, w]
                s = dot(kc, qts[h], 1, 1) * scale - lses[h]
                if masked:
                    s = jnp.where(seen, s, NEG)
                p = jnp.exp(s)
                dp = dot(v_s[krows, w], dos[h], 1, 1)
                ds = (p * (dp - deltas[h])).astype(jnp.bfloat16)
                dv_s[krows, w] += dot(p.astype(jnp.bfloat16), dos[h], 1, 0)
                dk_s[krows, w] += dot(ds, qts[h], 1, 0)
                out.append(accs[h] + dot(kc, ds, 0, 0))
            return tuple(out)

        accs = (jnp.zeros((head_size, rows), jnp.float32),) * heads
        accs = lax.fori_loop(0, full, functools.partial(step, masked=False), accs)
        accs = lax.fori_loop(full, last, functools.partial(step, masked=True), accs)
        for h, w in enumerate(windows):
            dq_s[pl.ds(base, rows), w] = (accs[h] * scale).T
        return carry

    lax.fori_loop(0, nq // per, tile_body, 0)
    v_s[...] = dv_s[...].astype(v_s.dtype)
    give(v_s, dv_refs, sems.at[4], blk, lambda i: kslot_ref[i])
    k_s[...] = (dk_s[...] * scale).astype(k_s.dtype)
    give(k_s, dk_refs, sems.at[3], blk, lambda i: kslot_ref[i])
    give(dq_s, [dq_ref], sems.at[0], blk, lambda i: place_ref[i])
    finish(v_s, sems.at[4])
    finish(k_s, sems.at[3])
    finish(dq_s, sems.at[0])


def attend_back(place, seq, kslot, q, ks, vs, o, do, lse, heads, head_size, blk):
    nq = q.shape[0] // blk
    per = min(4, nq)
    keys = sum(k.shape[0] for k in ks)
    bf16, f32 = q.dtype, jnp.float32
    out = pl.pallas_call(
        functools.partial(
            attend_back_kernel, heads=heads, head_size=head_size, blk=blk, per=per, chunk=512,
            scale=1.0 / math.sqrt(head_size), pieces=len(ks),
        ),
        out_shape=(
            jax.ShapeDtypeStruct(q.shape, f32),
            *(jax.ShapeDtypeStruct(k.shape, bf16) for k in ks),
            *(jax.ShapeDtypeStruct(v.shape, bf16) for v in vs),
        ),
        grid_spec=pltpu.PrefetchScalarGridSpec(
            num_scalar_prefetch=3,
            grid=(),
            in_specs=[ANY] * 3 + [WHOLE] + [ANY] * (2 * len(ks)),
            out_specs=[ANY] * (1 + 2 * len(ks)),
            scratch_shapes=[
                pltpu.VMEM(q.shape, bf16),
                pltpu.VMEM((keys, q.shape[1]), bf16),
                pltpu.VMEM((keys, q.shape[1]), bf16),
                pltpu.VMEM(q.shape, bf16),
                pltpu.VMEM(q.shape, bf16),
                pltpu.VMEM(q.shape, f32),
                pltpu.VMEM((keys, q.shape[1]), f32),
                pltpu.VMEM((keys, q.shape[1]), f32),
                pltpu.SemaphoreType.DMA((5,)),
            ],
        ),
        compiler_params=pltpu.CompilerParams(vmem_limit_bytes=60 * 1024 * 1024),
        name="attend_back",
    )(place, seq, kslot, q, o, do, lse, *ks, *vs)
    return out[0], out[1 : 1 + len(ks)], out[1 + len(ks) :]


def rotate(x, cosine, sine, heads, head_size):
    parts = []
    for h in range(heads):
        part = x[:, h * head_size : (h + 1) * head_size]
        parts.append(part * cosine + pltpu.roll(part, head_size // 2, 1) * sine)
    return jnp.concatenate(parts, axis=1)


def column(row):
    return jnp.broadcast_to(row, (8, row.shape[1])).T[:, :1]


def reciprocal_root(sums_ref, i, width):
    return column(lax.rsqrt(sums_ref[i : i + 1, :] / width + EPS))


def prepare_kernel(pre_ref, sums_ref, gain_ref, cos_ref, sin_ref, q_ref, k_ref, *, heads, head_size, width):
    wide = heads * head_size
    for i, out in enumerate((q_ref, k_ref)):
        recip = reciprocal_root(sums_ref, i, width)
        x = pre_ref[:, i * wide : (i + 1) * wide] * recip * gain_ref[i : i + 1, :]
        out[...] = rotate(x, cos_ref[...], sin_ref[...], heads, head_size).astype(out.dtype)


def by_row(step, n):
    return pl.BlockSpec((step, n), lambda i, *_: (i, 0))


def by_lane(step):
    return pl.BlockSpec((2, step), lambda i, *_: (0, i))


def fixed(rows, cols):
    return pl.BlockSpec((rows, cols), lambda i, *_: (0, 0))


TILE = 256


def prepare(pre, sums, gain, cosine, sine, heads, head_size, width):
    rows, wide = pre.shape[0], heads * head_size
    return pl.pallas_call(
        functools.partial(prepare_kernel, heads=heads, head_size=head_size, width=width),
        out_shape=(jax.ShapeDtypeStruct((rows, wide), jnp.bfloat16),) * 2,
        grid=(rows // TILE,),
        in_specs=[
            by_row(TILE, 2 * wide), by_lane(TILE), fixed(2, wide),
            by_row(TILE, head_size), by_row(TILE, head_size),
        ],
        out_specs=[by_row(TILE, wide)] * 2,
        name="prepare",
    )(pre, sums, gain, cosine, sine)


def unturn_kernel(
    dq_ref, dka_ref, dkb_ref, pre_ref, sums_ref, gain_ref, cos_ref, sin_ref,
    ds_ref, sum_ref, gg_ref, *, heads, head_size, width
):
    wide = heads * head_size
    dk = dka_ref[...] + dkb_ref[...].astype(jnp.float32)

    @pl.when(pl.program_id(0) == 0)
    def _():
        gg_ref[...] = jnp.zeros_like(gg_ref)

    for i, d in enumerate((dq_ref[...], dk)):
        cols = slice(i * wide, (i + 1) * wide)
        recip = reciprocal_root(sums_ref, i, width)
        n = rotate(d, cos_ref[...], -sin_ref[...], heads, head_size)
        pre = pre_ref[:, cols]
        gg_ref[i : i + 1, :] += jnp.sum(n * pre * recip, axis=0, keepdims=True)
        scaled = n * gain_ref[i : i + 1, :]
        ds_ref[:, cols] = scaled
        sum_ref[i : i + 1, :] = jnp.sum((scaled * pre).T, axis=0, keepdims=True)


def unturn(dq, dka, dkb, pre, sums, gain, cosine, sine, heads, head_size, width):
    rows, wide = pre.shape[0], heads * head_size
    return pl.pallas_call(
        functools.partial(unturn_kernel, heads=heads, head_size=head_size, width=width),
        out_shape=(
            jax.ShapeDtypeStruct((rows, 2 * wide), jnp.float32),
            jax.ShapeDtypeStruct((2, rows), jnp.float32),
            jax.ShapeDtypeStruct((2, wide), jnp.float32),
        ),
        grid=(rows // TILE,),
        in_specs=[
            by_row(TILE, wide), by_row(TILE, wide), by_row(TILE, wide), by_row(TILE, 2 * wide),
            by_lane(TILE), fixed(2, wide), by_row(TILE, head_size), by_row(TILE, head_size),
        ],
        out_specs=[by_row(TILE, 2 * wide), by_lane(TILE), fixed(2, wide)],
        name="unturn",
    )(dq, dka, dkb, pre, sums, gain, cosine, sine)


def fetch(refs, dst, sems):
    base = 0
    for ref in refs:
        rows = ref.shape[0]
        pltpu.make_async_copy(ref, dst.at[pl.ds(base, rows), :], sems.at[base // TILE]).start()
        base += rows


def arrive(dst, sems, tile):
    finish(dst.at[pl.ds(pl.multiple_of(tile * TILE, TILE), TILE), :], sems.at[tile])


def tile_rows(tile):
    return pl.ds(pl.multiple_of(tile * TILE, TILE), TILE)


def place_quarters(refs, dst, sem, cols, row_of):
    for j, ref in enumerate(refs):
        for s in range(ref.shape[0]):
            rows = ref.shape[1]
            row = pl.multiple_of(row_of(j // 2, j % 2, s) * rows, rows)
            pltpu.make_async_copy(ref.at[s, :, pl.ds(0, cols)], dst.at[pl.ds(row, rows), :], sem).start()


def project_kernel(me_ref, *refs, wide):
    x_refs, w_refs, refs = refs[:8], refs[8:12], refs[12:]
    pre_ref, v_ref, sum_ref, w_ref, x_s, x_sems, w_sem = refs
    tile = pl.program_id(0)

    @pl.when(tile == 0)
    def _():
        place_quarters(
            w_refs, w_ref, w_sem, 3 * wide,
            lambda jx, jy, s: (((s // 2) * 2 + (jy ^ me_ref[0])) * 2 + s % 2) * 2 + (jx ^ me_ref[1]),
        )
        fetch(x_refs, x_s, x_sems)
        finish(w_ref, w_sem)

    arrive(x_s, x_sems, tile)
    p = dot(x_s[tile_rows(tile), :], w_ref[...], 1, 0)
    pre_ref[...] = p[:, : 2 * wide]
    v_ref[...] = p[:, 2 * wide :].astype(v_ref.dtype)
    for i in range(2):
        part = p[:, i * wide : (i + 1) * wide]
        sum_ref[i : i + 1, :] = jnp.sum((part * part).T, axis=0, keepdims=True)


def project(me, xs, ws, wide):
    rows, d = xs[0].shape[0] * 8, xs[0].shape[1]
    bf16, f32 = xs[0].dtype, jnp.float32
    return pl.pallas_call(
        functools.partial(project_kernel, wide=wide),
        out_shape=(
            jax.ShapeDtypeStruct((rows, 2 * wide), f32),
            jax.ShapeDtypeStruct((rows, wide), bf16),
            jax.ShapeDtypeStruct((2, rows), f32),
            jax.ShapeDtypeStruct((d, 3 * wide), bf16),
        ),
        grid_spec=pltpu.PrefetchScalarGridSpec(
            num_scalar_prefetch=1,
            grid=(rows // TILE,),
            in_specs=[ANY] * 12,
            out_specs=[by_row(TILE, 2 * wide), by_row(TILE, wide), by_lane(TILE), fixed(d, 3 * wide)],
            scratch_shapes=[
                pltpu.VMEM((rows, d), bf16),
                pltpu.SemaphoreType.DMA((rows // TILE,)),
                pltpu.SemaphoreType.DMA,
            ],
        ),
        name="project",
    )(me, *xs, *ws)


def halves(tile, tiles, part, mine_ref, send_ref):
    @pl.when(tile < tiles // 2)
    def _():
        mine_ref[...] = part

    @pl.when(tile >= tiles // 2)
    def _():
        send_ref[...] = part.astype(send_ref.dtype)


def half_specs(tiles, cols):
    half = tiles // 2
    return [
        pl.BlockSpec((TILE, cols), lambda i, *_: (jnp.minimum(i, half - 1), 0)),
        pl.BlockSpec((TILE, cols), lambda i, *_: (jnp.maximum(i - half, 0), 0)),
    ]


def half_shapes(rows, cols):
    return [
        jax.ShapeDtypeStruct((rows // 2, cols), jnp.float32),
        jax.ShapeDtypeStruct((rows // 2, cols), jnp.bfloat16),
    ]


def expand_kernel(me_ref, *refs, units, tiles):
    x_refs, w_refs, d_refs, refs = refs[:8], refs[8:12], refs[12:16], refs[16:]
    gu_ref, hid_ref, mine_ref, send_ref, w_ref, d_ref, x_s, x_sems, w_sems = refs
    tile = pl.program_id(0)

    @pl.when(tile == 0)
    def _():
        place_quarters(
            w_refs, w_ref, w_sems.at[0], 2 * units,
            lambda jx, jh, s: (((s // 8) * 2 + (jh ^ me_ref[0])) * 8 + s % 8) * 2 + (jx ^ me_ref[1]),
        )
        fetch(x_refs, x_s, x_sems)
        place_quarters(
            d_refs, d_ref, w_sems.at[1], d_ref.shape[1],
            lambda jx, jh, s: (s * 2 + (jh ^ me_ref[0])) * 2 + (jx ^ me_ref[1]),
        )
        finish(w_ref, w_sems.at[0])

    arrive(x_s, x_sems, tile)
    p = dot(x_s[tile_rows(tile), :], w_ref[...], 1, 0)
    gu_ref[...] = p
    gate = p[:, :units]
    hidden = (gate * jax.nn.sigmoid(gate) * p[:, units:]).astype(hid_ref.dtype)
    hid_ref[...] = hidden

    @pl.when(tile == 0)
    def _():
        finish(d_ref, w_sems.at[1])

    halves(tile, tiles, dot(hidden, d_ref[...], 1, 0), mine_ref, send_ref)


def expand(me, xs, ws, ds, units):
    rows, d = xs[0].shape[0] * 8, xs[0].shape[1]
    tiles = rows // TILE
    bf16, f32 = xs[0].dtype, jnp.float32
    return pl.pallas_call(
        functools.partial(expand_kernel, units=units, tiles=tiles),
        out_shape=(
            jax.ShapeDtypeStruct((rows, 2 * units), f32),
            jax.ShapeDtypeStruct((rows, units), bf16),
            *half_shapes(rows, d),
            jax.ShapeDtypeStruct((d, 2 * units), bf16),
            jax.ShapeDtypeStruct((units, d), bf16),
        ),
        grid_spec=pltpu.PrefetchScalarGridSpec(
            num_scalar_prefetch=1,
            grid=(tiles,),
            in_specs=[ANY] * 16,
            out_specs=[
                by_row(TILE, 2 * units), by_row(TILE, units), *half_specs(tiles, d),
                fixed(d, 2 * units), fixed(units, d),
            ],
            scratch_shapes=[
                pltpu.VMEM((rows, d), bf16),
                pltpu.SemaphoreType.DMA((tiles,)),
                pltpu.SemaphoreType.DMA((2,)),
            ],
        ),
        name="expand",
    )(me, *xs, *ws, *ds)


def contract_kernel(gu_ref, w_ref, d_ref, *refs, units, tiles):
    x_refs, refs = refs[:8], refs[8:]
    dgu_ref, mine_ref, send_ref, x_s, x_sems = refs
    tile = pl.program_id(0)

    @pl.when(tile == 0)
    def _():
        fetch(x_refs, x_s, x_sems)

    arrive(x_s, x_sems, tile)
    dh = dot(x_s[tile_rows(tile), :], d_ref[...], 1, 1)
    gate, up = gu_ref[:, :units], gu_ref[:, units:]
    sig = jax.nn.sigmoid(gate)
    d_gate = (dh * up * sig * (1.0 + gate * (1.0 - sig))).astype(dgu_ref.dtype)
    d_up = (dh * (gate * sig)).astype(dgu_ref.dtype)
    dgu_ref[:, :units] = d_gate
    dgu_ref[:, units:] = d_up
    part = dot(d_gate, w_ref[:, :units], 1, 1) + dot(d_up, w_ref[:, units:], 1, 1)
    halves(tile, tiles, part, mine_ref, send_ref)


def contract(gu, w_gu, w_d, xs):
    units, d = w_d.shape
    rows = gu.shape[0]
    tiles = rows // TILE
    bf16 = w_d.dtype
    return pl.pallas_call(
        functools.partial(contract_kernel, units=units, tiles=tiles),
        out_shape=(jax.ShapeDtypeStruct((rows, 2 * units), bf16), *half_shapes(rows, d)),
        grid=(tiles,),
        in_specs=[by_row(TILE, 2 * units), fixed(d, 2 * units), fixed(units, d)] + [ANY] * 8,
        out_specs=[by_row(TILE, 2 * units), *half_specs(tiles, d)],
        scratch_shapes=[pltpu.VMEM((rows, d), bf16), pltpu.SemaphoreType.DMA((tiles,))],
        name="contract",
    )(gu, w_gu, w_d, *xs)


def outer_halves(a, b, me, keep_ref, send_ref):
    half = a.shape[1] // 2
    window = lambda i: a[:, pl.ds(pl.multiple_of(i * half, half), half)]
    keep_ref[...] = dot(window(me), b[...], 0, 0)
    send_ref[...] = dot(window(1 - me), b[...], 0, 0).astype(send_ref.dtype)


def grads_kernel(me_ref, hid_ref, dgu_ref, *refs):
    x_refs, g_refs, refs = refs[:8], refs[8:16], refs[16:]
    keep_gu, send_gu, keep_d, send_d, x_s, g_s, sems = refs
    base = 0
    for x_ref, g_ref in zip(x_refs, g_refs):
        rows = x_ref.shape[0]
        pltpu.make_async_copy(x_ref, x_s.at[pl.ds(base, rows), :], sems.at[0]).start()
        pltpu.make_async_copy(g_ref, g_s.at[pl.ds(base, rows), :], sems.at[1]).start()
        base += rows
    finish(x_s, sems.at[0])
    outer_halves(x_s, dgu_ref, me_ref[0], keep_gu, send_gu)
    finish(g_s, sems.at[1])
    outer_halves(hid_ref, g_s, me_ref[0], keep_d, send_d)


def split_shapes(rows, cols):
    return [
        jax.ShapeDtypeStruct((rows // 2, cols), jnp.float32),
        jax.ShapeDtypeStruct((rows // 2, cols), jnp.bfloat16),
    ]


def grads(me, hidden, d_gu, xs, gs):
    rows, units = hidden.shape
    d = xs[0].shape[1]
    bf16 = hidden.dtype
    return pl.pallas_call(
        grads_kernel,
        out_shape=(*split_shapes(d, 2 * units), *split_shapes(units, d)),
        grid_spec=pltpu.PrefetchScalarGridSpec(
            num_scalar_prefetch=1,
            grid=(),
            in_specs=[WHOLE, WHOLE] + [ANY] * 16,
            out_specs=[WHOLE] * 4,
            scratch_shapes=[
                pltpu.VMEM((rows, d), bf16),
                pltpu.VMEM((rows, d), bf16),
                pltpu.SemaphoreType.DMA((2,)),
            ],
        ),
        compiler_params=pltpu.CompilerParams(vmem_limit_bytes=40 * 1024 * 1024),
        name="grads",
    )(me, hidden, d_gu, *xs, *gs)


def project_back_kernel(me_ref, o_ref, w_ref, *refs):
    g_refs, refs = refs[:8], refs[8:]
    do_ref, keep_ref, send_ref, g_s, sem = refs
    base = 0
    for g_ref in g_refs:
        pltpu.make_async_copy(g_ref, g_s.at[pl.ds(base, g_ref.shape[0]), :], sem).start()
        base += g_ref.shape[0]
    finish(g_s, sem)
    do_ref[...] = dot(g_s[...], w_ref[...], 1, 1).astype(do_ref.dtype)
    outer_halves(o_ref, g_s, me_ref[0], keep_ref, send_ref)


def project_back(me, attended, w_o, gs):
    rows, wide = attended.shape
    d = w_o.shape[1]
    bf16 = w_o.dtype
    return pl.pallas_call(
        project_back_kernel,
        out_shape=(jax.ShapeDtypeStruct((rows, wide), bf16), *split_shapes(wide, d)),
        grid_spec=pltpu.PrefetchScalarGridSpec(
            num_scalar_prefetch=1,
            grid=(),
            in_specs=[WHOLE, WHOLE] + [ANY] * 8,
            out_specs=[WHOLE] * 3,
            scratch_shapes=[pltpu.VMEM((rows, d), bf16), pltpu.SemaphoreType.DMA],
        ),
        name="project_back",
    )(me, attended, w_o, *gs)


def norms_back_kernel(
    me_ref, ds_ref, sums_ref, dsums_ref, pre_ref, dva_ref, dvb_ref, *refs, wide, width, tiles
):
    x_refs, refs = refs[:8], refs[8:]
    dqkv_ref, keep_ref, send_ref, x_s, acc_s, x_sems = refs
    tile = pl.program_id(0)

    @pl.when(tile == 0)
    def _():
        fetch(x_refs, x_s, x_sems)
        acc_s[...] = jnp.zeros_like(acc_s)

    for i in range(2):
        cols = slice(i * wide, (i + 1) * wide)
        recip = reciprocal_root(sums_ref, i, width)
        total = column(dsums_ref[i : i + 1, :])
        value = recip * ds_ref[:, cols] - pre_ref[:, cols] * (recip * recip * recip) * total / width
        dqkv_ref[:, cols] = value.astype(dqkv_ref.dtype)
    dv = dva_ref[...] + dvb_ref[...].astype(jnp.float32)
    dqkv_ref[:, 2 * wide :] = dv.astype(dqkv_ref.dtype)
    arrive(x_s, x_sems, tile)
    acc_s[...] += dot(x_s[tile_rows(tile), :], dqkv_ref[...], 0, 0)

    @pl.when(tile == tiles - 1)
    def _():
        half = acc_s.shape[0] // 2
        window = lambda i: acc_s[pl.ds(pl.multiple_of(i * half, half), half), :]
        keep_ref[...] = window(me_ref[0])
        send_ref[...] = window(1 - me_ref[0]).astype(send_ref.dtype)


def norms_back(me, d_scaled, sums, dsums, pre, dva, dvb, xs, width):
    rows, wide = dva.shape
    d = xs[0].shape[1]
    tiles = rows // TILE
    bf16 = jnp.bfloat16
    half = d // 2
    return pl.pallas_call(
        functools.partial(norms_back_kernel, wide=wide, width=width, tiles=tiles),
        out_shape=(jax.ShapeDtypeStruct((rows, 3 * wide), bf16), *split_shapes(d, 3 * wide)),
        grid_spec=pltpu.PrefetchScalarGridSpec(
            num_scalar_prefetch=1,
            grid=(tiles,),
            in_specs=[
                by_row(TILE, 2 * wide), by_lane(TILE), by_lane(TILE), by_row(TILE, 2 * wide),
                by_row(TILE, wide), by_row(TILE, wide),
            ] + [ANY] * 8,
            out_specs=[by_row(TILE, 3 * wide), fixed(half, 3 * wide), fixed(half, 3 * wide)],
            scratch_shapes=[
                pltpu.VMEM((rows, d), bf16),
                pltpu.VMEM((d, 3 * wide), jnp.float32),
                pltpu.SemaphoreType.DMA((tiles,)),
            ],
        ),
        name="norms_back",
    )(me, d_scaled, sums, dsums, pre, dva, dvb, *xs)


def inputs_back_kernel(g_ref, w_ref, mine_ref, send_ref, *, tiles):
    halves(pl.program_id(0), tiles, dot(g_ref[...], w_ref[...], 1, 1), mine_ref, send_ref)


def inputs_back(g, w):
    rows, cols = g.shape
    d = w.shape[0]
    tiles = rows // TILE
    return pl.pallas_call(
        functools.partial(inputs_back_kernel, tiles=tiles),
        out_shape=tuple(half_shapes(rows, d)),
        grid=(tiles,),
        in_specs=[by_row(TILE, cols), fixed(d, cols)],
        out_specs=half_specs(tiles, d),
        name="inputs_back",
    )(g, w)


def unpack_kernel(src_ref, *refs, plan, pieces, cover):
    outs = refs[: len(plan[0])]
    got, wide, in_sems, out_sems = refs[len(outs) :]

    def fetch(p):
        return pltpu.make_async_copy(src_ref.at[p], got.at[p % 2], in_sems.at[p % 2])

    def parts(p):
        copies = []
        for out, moves in zip(outs, plan[p]):
            for rows, cols, drow, dcol in moves:
                copies.append(
                    pltpu.make_async_copy(
                        wide.at[p % 2, pl.ds(*rows), pl.ds(*cols)],
                        out.at[pl.ds(drow, rows[1]), pl.ds(dcol, cols[1])],
                        out_sems.at[p % 2],
                    )
                )
        return copies

    def done(p):
        window = wide.at[p % 2, pl.ds(0, cover), :]
        pltpu.make_async_copy(window, window, out_sems.at[p % 2]).wait()

    fetch(0).start()
    for p in range(pieces):
        if p + 1 < pieces:
            fetch(p + 1).start()
        fetch(p).wait()
        if p >= 2:
            done(p - 2)
        wide[p % 2] = got[p % 2].astype(jnp.float32)
        for copy in parts(p):
            copy.start()
    for p in range(max(pieces - 2, 0), pieces):
        done(p)


def unpack(src, shapes, plan, cover):
    pieces, rows, cols = src.shape
    return pl.pallas_call(
        functools.partial(unpack_kernel, plan=plan, pieces=pieces, cover=cover),
        out_shape=tuple(jax.ShapeDtypeStruct(s, jnp.float32) for s in shapes),
        in_specs=[ANY],
        out_specs=[ANY] * len(shapes),
        scratch_shapes=[
            pltpu.VMEM((2, rows, cols), src.dtype),
            pltpu.VMEM((2, rows, cols), jnp.float32),
            pltpu.SemaphoreType.DMA((2,)),
            pltpu.SemaphoreType.DMA((2,)),
        ],
        compiler_params=pltpu.CompilerParams(vmem_limit_bytes=40 * 1024 * 1024),
        name="unpack",
    )(src)


THETA = 500000.0
HD = 128


def norm_forward(value, gain):
    recip = lax.rsqrt(jnp.mean(value * value, axis=-1, keepdims=True) + EPS)
    return (value * recip * gain, recip)


def norm_backward(value, recip, gain, grad_out):
    scaled = grad_out * gain
    width = value.shape[-1]
    grad_in = (
        recip * scaled
        - value * (recip * recip * recip) * jnp.sum(scaled * value, axis=-1, keepdims=True) / width
    )
    grad_gain = jnp.sum(grad_out * value * recip, axis=0)
    return (grad_in, grad_gain)


def flip(value, *axes):
    last = 2 ** len(axes) - 1
    return lax.ppermute(value, axes, [(i, i ^ last) for i in range(last + 1)])


def after(value, *others):
    return lax.optimization_barrier((value, others))[0]


def gather8(x, a, b):
    own = [x, flip(x, b), flip(x, a), flip(x, a, b)]
    return own + [flip(v, "c") for v in own]


def scatter8(own, send, a, b):
    f32, bf16 = jnp.float32, jnp.bfloat16
    own = (own + flip(send, "c").astype(f32)).reshape(4, own.shape[0] // 4, own.shape[1])
    out = own.astype(bf16)
    return (
        own[0]
        + flip(out[1], b).astype(f32)
        + flip(out[2], a).astype(f32)
        + flip(out[3], a, b).astype(f32)
    )


def sum8(x, a, b):
    t = x.reshape(2, 8, -1)
    for bit, name in ((4, "c"), (2, a), (1, b)):
        got = flip(t.reshape(16, -1), name).reshape(t.shape)
        t = t + jnp.concatenate([got[:, k ^ bit : (k ^ bit) + 1] for k in range(8)], axis=1)
    return t.reshape(x.shape)


def in_order(value, axis, name):
    return jnp.where(lax.axis_index(name) == 1, jnp.flip(value, axis), value)


def quarters(x, a, b):
    first = flip(x, a)
    return [x, first, flip(x, b), flip(first, b)]


def gather4(x, a, b):
    quad = jnp.stack(quarters(x, a, b)).reshape((2, 2) + x.shape)
    return in_order(in_order(quad, 1, a), 0, b)


def halve(x, name):
    me = lax.axis_index(name)
    keep = lax.dynamic_index_in_dim(x, me, 0, keepdims=False)
    send = lax.dynamic_index_in_dim(x, 1 - me, 0, keepdims=False)
    return keep.astype(jnp.float32) + flip(send.astype(jnp.bfloat16), name).astype(jnp.float32)


def layer(
    layer_input,
    grad_output,
    positions,
    w_query,
    w_key,
    w_value,
    w_out,
    w_gate,
    w_up,
    w_down,
    gain_query,
    gain_key,
    gain_attn,
    gain_mlp,
    *,
    outer,
):
    f32 = jnp.float32
    bf16 = jnp.bfloat16
    rows, d = layer_input.shape
    drows, e = w_query.shape
    f = w_gate.shape[1]
    blk = rows // 2
    devices = positions.shape[0] // rows
    teams = devices // 8
    every = ("o", "h", "l", "y", "c", "x")
    heads = e // HD
    mine = heads // 8
    wide = mine * HD
    index = {name: lax.axis_index(name) for name in every}

    def by_team(w):
        return w.reshape(drows, mine, 8, HD).transpose(2, 0, 1, 3).reshape(8, drows, wide)

    gains = jnp.concatenate([gain_query, gain_key, gain_attn, gain_mlp])
    pad = drows * 128 - gains.shape[0]
    gains = jnp.pad(gains, (0, pad)).reshape(1, drows, 128)
    payload = jnp.concatenate(
        [by_team(w_query), by_team(w_key), by_team(w_value), jnp.broadcast_to(gains, (8, drows, 128))],
        axis=2,
    )
    payload = lax.all_to_all(payload, ("h", "l", "c"), 0, 0, tiled=True)
    w_pieces = quarters(payload, "y", "x")
    gains = jnp.stack([p[:, :, 3 * wide :] for p in w_pieces])
    if outer > 1:
        w_pieces = [lax.all_gather(p, "o", axis=0, tiled=True) for p in w_pieces]
        gains = lax.all_gather(gains, "o", axis=0)
    gains = gains.reshape(outer, 2, 2, 2, 2, 2, drows * 128)
    gains = in_order(in_order(gains, 2, "y"), 1, "x").transpose(0, 3, 4, 2, 5, 1, 6)
    gains = gains.reshape(devices, drows * 128)
    e_own, d_own = e // devices, d // devices
    full_gq = gains[:, :e_own].reshape(e)
    full_gk = gains[:, e_own : 2 * e_own].reshape(e)
    full_ga = gains[:, 2 * e_own : 2 * e_own + d_own].reshape(1, d).astype(f32)
    full_gm = gains[:, 2 * e_own + d_own : 2 * e_own + 2 * d_own].reshape(1, d).astype(f32)
    team_a = index["h"] * 4 + index["l"] * 2 + index["c"]

    def own_gain(g):
        return lax.dynamic_index_in_dim(g.reshape(mine, 8, HD), team_a, 1, keepdims=False).reshape(wide)

    gain_qk = jnp.stack([own_gain(full_gq), own_gain(full_gk)]).astype(f32)

    if outer == 1:
        w_o = gather4(w_out, "h", "x").transpose(1, 0, 2, 3).reshape(wide, d)
        w_o = lax.ppermute(
            w_o, ("h", "l", "y"), [(i, 2 * (i % 4) + i // 4) for i in range(8)]
        )
    else:
        w_o = lax.all_gather(w_out, every, axis=0, tiled=True).reshape(mine, 8, HD, d)
        w_o = lax.dynamic_index_in_dim(w_o, team_a, 1, keepdims=False).reshape(wide, d)

    unit = f // (8 * outer * 2)
    units = outer * 2 * unit

    def by_unit(w):
        return w.reshape(drows, outer * 2, 8, unit).transpose(2, 0, 1, 3).reshape(8, drows, units)

    ff = after(jnp.concatenate([by_unit(w_gate), by_unit(w_up)], axis=2), payload)
    ff = lax.all_to_all(ff, ("l", "y", "c"), 0, 0, tiled=True)
    f_pieces = quarters(ff, "h", "x")
    d_pieces = quarters(w_down[None], "h", "x")
    if outer > 1:
        f_pieces = [lax.all_gather(p, "o", axis=0, tiled=True) for p in f_pieces]
        d_pieces = [lax.all_gather(p, "o", axis=0, tiled=True) for p in d_pieces]

    table = positions.reshape(outer, 2, 2, 2, 2, 2, rows)[..., ::blk] // blk
    for axis, name in enumerate(every):
        if name != "o":
            table = in_order(table, axis, name)
    kslot = table.transpose(0, 5, 3, 4, 1, 2, 6)
    qblocks = lax.dynamic_index_in_dim(kslot, index["o"], 0, keepdims=False)[0, 0].reshape(-1)
    kslot = kslot.reshape(-1)
    nq = qblocks.shape[0]
    place = jnp.sum((qblocks[None, :] < qblocks[:, None]).astype(jnp.int32), axis=1)
    seq = jnp.sum(
        jnp.where(place[None, :] == jnp.arange(nq)[:, None], qblocks[None, :], 0), axis=1
    ).astype(jnp.int32)
    group_pos = (qblocks[:, None] * blk + jnp.arange(blk, dtype=jnp.int32)[None, :]).reshape(-1)
    freqs = THETA ** (-(2.0 * jnp.arange(HD // 2, dtype=f32)) / HD)
    angles = group_pos.astype(f32)[:, None] * freqs[None, :]
    cosine, sine = jnp.cos(angles), jnp.sin(angles)
    cosine = jnp.concatenate([cosine, cosine], axis=1)
    sine = jnp.concatenate([-sine, sine], axis=1)

    me_yx = jnp.stack([index["y"], index["x"]]).astype(jnp.int32)
    me_hx = jnp.stack([index["h"], index["x"]]).astype(jnp.int32)
    me_x = me_yx[1:]
    xs = gather8(layer_input.astype(bf16), "h", "l")
    group = 8 * rows
    pre, value, squares, w_qkv = project(me_yx, xs, w_pieces, wide)
    squares = sum8(squares, "h", "l")
    query, key = prepare(pre, squares, gain_qk, cosine, sine, mine, HD, e)
    key_y, value_x = flip(key, "y"), flip(value, "x")
    keys = [key, key_y, flip(key, "x"), flip(key_y, "x")]
    values = [value, flip(value, "y"), value_x, flip(value_x, "y")]
    if outer > 1:
        keys = [lax.all_gather(jnp.stack(keys), "o", axis=0).reshape(-1, wide)]
        values = [lax.all_gather(jnp.stack(values), "o", axis=0).reshape(-1, wide)]
    query = after(query, f_pieces, d_pieces)
    attended, lse, own, send = attend(place, seq, kslot, query, keys, values, w_o, mine, HD, blk)
    proj = scatter8(own, send, "h", "l")
    attn_branch, a_recip = norm_forward(proj, full_ga)
    mid = layer_input + attn_branch

    ms = gather8(mid.astype(bf16), "l", "y")
    gate_up, hidden, own, send, w_gu, w_d = expand(me_hx, ms, f_pieces, d_pieces, units)
    down = scatter8(own, send, "l", "y")
    mlp_branch, m_recip = norm_forward(down, full_gm)
    output = mid + mlp_branch
    d_down_f, local_gm = norm_backward(down, m_recip, full_gm, grad_output)
    dgs = gather8(d_down_f.astype(bf16), "l", "y")
    d_gu, own, send = contract(gate_up, w_gu, w_d, dgs)
    d_mid = grad_output + scatter8(own, send, "l", "y")
    keep_gu, send_gu, keep_d, send_d = grads(me_x, hidden, d_gu, ms, dgs)

    ctx = ("o", "h", "l", "y", "c")

    def settle(keep, send, a):
        cols = keep.shape[1]
        part = keep + flip(send, "x").astype(f32)
        part = halve(part.reshape(2, -1, cols), a)
        if outer > 1:
            part = lax.psum_scatter(
                part.astype(bf16).reshape(outer, -1, cols), "o", scatter_dimension=0, tiled=False
            )
        return part.astype(bf16)

    part_gu, part_d = settle(keep_gu, send_gu, "h"), settle(keep_d, send_d, "h")
    part_f = jnp.concatenate([part_gu, part_d]) if outer == 1 else part_gu

    d_proj_f, local_ga = norm_backward(proj, a_recip, full_ga, d_mid)
    pgs = gather8(d_proj_f.astype(bf16), "h", "l")
    d_att, keep_o, send_o = project_back(me_x, attended, w_o, pgs)
    d_att = after(d_att, part_f)
    if outer == 1:
        first = lax.all_gather(part_f, ctx, axis=0).reshape(16, -1, d)
    dq_rot, dk, dv = attend_back(
        place, seq, kslot, query, keys, values, attended, d_att, lse, mine, HD, blk
    )
    if outer > 1:
        def own_quarter(g):
            g = g[0].reshape(outer, 4, group, wide)
            return list(lax.psum_scatter(g, "o", scatter_dimension=0, tiled=False))

        dk, dv = own_quarter(dk), own_quarter(dv)
    dk_a = dk[0].astype(f32) + flip(dk[2], "x").astype(f32)
    dk_b = flip((dk[1].astype(f32) + flip(dk[3], "x").astype(f32)).astype(bf16), "y")
    dv_a = dv[0].astype(f32) + flip(dv[1], "y").astype(f32)
    dv_b = flip((dv[2].astype(f32) + flip(dv[3], "y").astype(f32)).astype(bf16), "x")
    d_scaled, dsums, local_gqk = unturn(
        dq_rot, dk_a, dk_b, pre, squares, gain_qk, cosine, sine, mine, HD, e
    )
    dsums = sum8(dsums, "h", "l")
    d_qkv, keep_qkv, send_qkv = norms_back(me_x, d_scaled, squares, dsums, pre, dv_a, dv_b, xs, e)
    own, send = inputs_back(d_qkv, w_qkv)
    grad_input = d_mid + scatter8(own, send, "h", "l")

    half_d, half_f = d // 2, f // 2
    part_o, part_qkv = settle(keep_o, send_o, "y"), settle(keep_qkv, send_qkv, "y")
    n_qk, n_am = wide, d
    lines = -(-max(n_qk, n_am) // (3 * wide))
    lines = -(-lines // 16) * 16

    def line(v, n):
        return jnp.pad(v.reshape(2, n), ((0, 0), (0, lines * 3 * wide - n)))

    small = jnp.stack(
        [
            line(local_gqk.reshape(2, 2, -1).transpose(1, 0, 2), n_qk),
            line(jnp.stack([local_ga, local_gm]).reshape(2, 2, -1).transpose(1, 0, 2), n_am),
        ],
        axis=1,
    )
    small = halve(small, "x")
    small = halve(small, "y")
    if outer > 1:
        small = lax.psum(small, "o") / outer
    small = small.reshape(lines, 3 * wide).astype(bf16)
    part_qkv = jnp.concatenate([part_qkv, small])
    n_gu, n_d, n_o, n_qkv = part_gu.shape[0], part_d.shape[0], part_o.shape[0], part_qkv.shape[0] - lines

    if outer == 1:
        part_qkv = after(part_qkv, first)
        middle = lax.all_gather(after(part_o, first), ctx, axis=0).reshape(16, -1, d)
        last = lax.all_gather(part_qkv, ctx, axis=0).reshape(16, -1, 3 * wide)
        plan_first, plan_middle, plan_last = [], [], []
        for p in range(16):
            h, l, y, c = p >> 3, (p >> 2) & 1, (p >> 1) & 1, p & 1
            team_f, team_q = 4 * l + 2 * y + c, 4 * h + 2 * l + c
            ups = [
                [
                    ((0, n_gu), (m * units + o * unit, unit), h * n_gu, (o * 8 + team_f) * unit)
                    for o in range(2)
                ]
                for m in range(2)
            ]
            downs = [((n_gu, n_d), (0, d), team_f * unit + h * n_d, 0)]
            plan_first.append([*ups, downs])
            plan_middle.append([[((0, n_o), (0, d), team_q * HD + y * n_o, 0)]])
            plan_last.append(
                [
                    [
                        ((0, n_qkv), (m * wide + o * HD, HD), y * n_qkv, (o * 8 + team_q) * HD)
                        for o in range(mine)
                    ]
                    for m in range(3)
                ]
            )
        total_wg, total_wu, total_wd = unpack(
            first, [(half_d, f), (half_d, f), (half_f, d)], plan_first, n_gu + n_d
        )
        (total_wo,) = unpack(middle, [(e // 2, d)], plan_middle, n_o)
        total_wq, total_wk, total_wv = unpack(last, [(half_d, e)] * 3, plan_last, n_qkv)
        got_small = last[:, n_qkv:]
    else:
        got = lax.all_gather(part_qkv, ctx, axis=0)
        got_small = got.reshape(-1, n_qkv + lines, 3 * wide)[:, n_qkv:]
        got = got.reshape(outer, 2, 2, 2, 2, n_qkv + lines, 3 * wide)[..., :n_qkv, :]
        got = got.transpose(3, 0, 5, 1, 2, 4, 6).reshape(half_d, 8, 3, mine, HD)
        got = got.transpose(2, 0, 3, 1, 4).reshape(3, half_d, e)
        total_wq, total_wk, total_wv = got[0].astype(f32), got[1].astype(f32), got[2].astype(f32)
        got = lax.all_gather(part_gu, ctx, axis=0)
        got = got.reshape(outer, 2, 8, n_gu, 2, outer * 2, unit)
        got = got.transpose(4, 1, 0, 3, 5, 2, 6).reshape(2, half_d, f)
        total_wg, total_wu = got[0].astype(f32), got[1].astype(f32)
        got = lax.all_gather(part_d, ctx, axis=0)
        got = got.reshape(outer, 2, 8, n_d, d).transpose(2, 1, 0, 3, 4)
        total_wd = got.reshape(8, outer, unit, d).transpose(1, 0, 2, 3).reshape(half_f, d).astype(f32)
        got = lax.all_gather(part_o, ctx, axis=0)
        got = got.reshape(outer, 2, 2, 2, 2, n_o, d).transpose(1, 2, 4, 3, 0, 5, 6)
        total_wo = got.reshape(e // 2, d).astype(f32)

    got_small = got_small.astype(f32).reshape(outer, 4, 2, 2, lines * 3 * wide)
    if outer > 1:
        got_small = jnp.sum(got_small, axis=0)
    else:
        got_small = got_small[0]
    qk = got_small[:, 0, :, :n_qk].reshape(8, 2, mine // 2, HD).transpose(1, 2, 0, 3).reshape(2, e // 2)
    total_gq, total_gk = qk[0], qk[1]
    am = jnp.sum(got_small[:, 1, :, :n_am], axis=(0, 1)).reshape(2, half_d)
    total_ga, total_gm = am[0], am[1]
    return (
        output,
        grad_input,
        total_wq,
        total_wk,
        total_wv,
        total_wo,
        total_wg,
        total_wu,
        total_wd,
        total_gq,
        total_gk,
        total_ga,
        total_gm,
    )


def solution(mesh):
    outer = mesh.shape["ctx"] // 16
    names = ("o", "h", "l", "y", "c", "x")
    fine = Mesh(mesh.devices.reshape(outer, 2, 2, 2, 2, 2), names)
    every, half = P(names), P("x")
    in_specs = (every, every, P()) + (every,) * 11
    out_specs = (every, every) + (half,) * 11
    return jax.shard_map(
        functools.partial(layer, outer=outer),
        mesh=fine,
        in_specs=in_specs,
        out_specs=out_specs,
        check_vma=False,
    )
```

```python
import functools
import math

import jax
import jax.numpy as jnp
from jax import lax
from jax.experimental import pallas as pl
from jax.experimental.pallas import tpu as pltpu
from jax.sharding import Mesh
from jax.sharding import PartitionSpec as P

EPS = 1e-06
NEG = -1e30


def dot(a, b, ca, cb):
    return lax.dot_general(a, b, (((ca,), (cb,)), ((), ())), preferred_element_type=jnp.float32)


def query_positions(seq_ref, tile, per, blk):
    lane = lax.broadcasted_iota(jnp.int32, (1, per * blk), 1)
    out = jnp.zeros((1, per * blk), jnp.int32)
    for b in range(per):
        first = seq_ref[tile * per + b] * blk
        out = jnp.where(lane // blk == b, first + lane - b * blk, out)
    return out


def sorted_load(src, dst, sem, count, blk, slot):
    def start(i, carry):
        pltpu.make_async_copy(
            src.at[pl.ds(pl.multiple_of(i * blk, blk), blk), :],
            dst.at[pl.ds(pl.multiple_of(slot(i) * blk, blk), blk), :],
            sem,
        ).start()
        return carry

    lax.fori_loop(0, count, start, 0)


def take(srcs, dst, sem, blk, slot):
    base = 0
    for src in srcs:
        sorted_load(src, dst, sem, src.shape[0] // blk, blk, lambda i, base=base: slot(base + i))
        base += src.shape[0] // blk


def finish(dst, sem):
    pltpu.make_async_copy(dst, dst, sem).wait()


def give(src, dsts, sem, blk, slot):
    base = 0
    for dst in dsts:

        def start(i, carry, dst=dst, base=base):
            pltpu.make_async_copy(
                src.at[pl.ds(pl.multiple_of(slot(base + i) * blk, blk), blk), :],
                dst.at[pl.ds(pl.multiple_of(i * blk, blk), blk), :],
                sem,
            ).start()
            return carry

        lax.fori_loop(0, dst.shape[0] // blk, start, 0)
        base += dst.shape[0] // blk


def attend_kernel(place_ref, seq_ref, kslot_ref, *refs, heads, head_size, blk, per, chunk, scale, pieces):
    (q_ref, wo_ref), refs = refs[:2], refs[2:]
    k_refs, v_refs, refs = refs[:pieces], refs[pieces : 2 * pieces], refs[2 * pieces :]
    o_ref, lse_ref, mine_ref, send_ref, q_s, k_s, v_s, o_s, wo_s, part_s, low_s, sems = refs
    nq = q_s.shape[0] // blk
    rows = per * blk
    take([q_ref], q_s, sems.at[0], blk, lambda i: place_ref[i])
    take(k_refs, k_s, sems.at[1], blk, lambda i: kslot_ref[i])
    take(v_refs, v_s, sems.at[2], blk, lambda i: kslot_ref[i])
    pltpu.make_async_copy(wo_ref, wo_s, sems.at[3]).start()
    finish(q_s, sems.at[0])
    finish(k_s, sems.at[1])
    finish(v_s, sems.at[2])
    finish(wo_s, sems.at[3])

    def tile_body(tile, carry):
        base = pl.multiple_of(tile * rows, rows)
        qpos = query_positions(seq_ref, tile, per, blk)
        full = (seq_ref[tile * per] * blk) // chunk
        last = ((seq_ref[tile * per + per - 1] + 1) * blk + chunk - 1) // chunk
        windows = [pl.ds(h * head_size, head_size) for h in range(heads)]
        qts = [q_s[pl.ds(base, rows), w] for w in windows]

        def step(j, states, masked):
            low = pl.multiple_of(j * chunk, chunk)
            krows = pl.ds(low, chunk)
            if masked:
                kpos = low + lax.broadcasted_iota(jnp.int32, (chunk, rows), 0)
                seen = kpos <= qpos
            scores = [dot(k_s[krows, w], qt, 1, 1) * scale for w, qt in zip(windows, qts)]
            out = []
            for w, s, (top, total, acc) in zip(windows, scores, states):
                if masked:
                    s = jnp.where(seen, s, NEG)
                top_new = jnp.maximum(top, jnp.max(s, axis=0, keepdims=True))
                p = jnp.exp(s - top_new)
                factor = jnp.exp(top - top_new)
                total = total * factor + jnp.sum(p, axis=0, keepdims=True)
                acc = acc * factor + dot(v_s[krows, w], p.astype(jnp.bfloat16), 0, 0)
                out.append((top_new, total, acc))
            return tuple(out)

        state = (
            jnp.full((1, rows), NEG, jnp.float32),
            jnp.zeros((1, rows), jnp.float32),
            jnp.zeros((head_size, rows), jnp.float32),
        )
        states = (state,) * heads
        states = lax.fori_loop(0, full, functools.partial(step, masked=False), states)
        states = lax.fori_loop(full, last, functools.partial(step, masked=True), states)
        for h, (top, total, acc) in enumerate(states):
            o_s[pl.ds(base, rows), windows[h]] = (acc / total).T.astype(o_s.dtype)
            lse_ref[pl.ds(tile * heads + h, 1), :] = top + jnp.log(total)
        part = dot(o_s[pl.ds(base, rows), :], wo_s[...], 1, 0)
        part_s[pl.ds(base, rows), :] = part
        low_s[pl.ds(base, rows), :] = part.astype(low_s.dtype)
        return carry

    lax.fori_loop(0, nq // per, tile_body, 0)
    half = nq // 2
    give(part_s, [mine_ref], sems.at[1], blk, lambda i: place_ref[i])
    give(low_s, [send_ref], sems.at[2], blk, lambda i: place_ref[half + i])
    give(o_s, [o_ref], sems.at[0], blk, lambda i: place_ref[i])
    finish(mine_ref, sems.at[1])
    finish(send_ref, sems.at[2])
    finish(o_s, sems.at[0])


ANY = pl.BlockSpec(memory_space=pl.ANY)
WHOLE = pl.BlockSpec(memory_space=pltpu.VMEM)


def attend(place, seq, kslot, q, ks, vs, w_o, heads, head_size, blk):
    nq = q.shape[0] // blk
    per = min(4, nq)
    rows = per * blk
    keys = sum(k.shape[0] for k in ks)
    return pl.pallas_call(
        functools.partial(
            attend_kernel, heads=heads, head_size=head_size, blk=blk, per=per, chunk=512,
            scale=1.0 / math.sqrt(head_size), pieces=len(ks),
        ),
        out_shape=(
            jax.ShapeDtypeStruct(q.shape, q.dtype),
            jax.ShapeDtypeStruct((nq // per * heads, rows), jnp.float32),
            jax.ShapeDtypeStruct((q.shape[0] // 2, w_o.shape[1]), jnp.float32),
            jax.ShapeDtypeStruct((q.shape[0] // 2, w_o.shape[1]), q.dtype),
        ),
        grid_spec=pltpu.PrefetchScalarGridSpec(
            num_scalar_prefetch=3,
            grid=(),
            in_specs=[ANY] * (2 + 2 * len(ks)),
            out_specs=[ANY, WHOLE, ANY, ANY],
            scratch_shapes=[
                pltpu.VMEM(q.shape, q.dtype),
                pltpu.VMEM((keys, q.shape[1]), q.dtype),
                pltpu.VMEM((keys, q.shape[1]), q.dtype),
                pltpu.VMEM(q.shape, q.dtype),
                pltpu.VMEM(w_o.shape, q.dtype),
                pltpu.VMEM((q.shape[0], w_o.shape[1]), jnp.float32),
                pltpu.VMEM((q.shape[0], w_o.shape[1]), q.dtype),
                pltpu.SemaphoreType.DMA((4,)),
            ],
        ),
        compiler_params=pltpu.CompilerParams(vmem_limit_bytes=58 * 1024 * 1024),
        name="attend",
    )(place, seq, kslot, q, w_o, *ks, *vs)


def attend_back_kernel(
    place_ref, seq_ref, kslot_ref, *refs, heads, head_size, blk, per, chunk, scale, pieces
):
    (q_ref, o_ref, do_ref, lse_ref), refs = refs[:4], refs[4:]
    k_refs, v_refs, refs = refs[:pieces], refs[pieces : 2 * pieces], refs[2 * pieces :]
    dq_ref, refs = refs[0], refs[1:]
    dk_refs, dv_refs, refs = refs[:pieces], refs[pieces : 2 * pieces], refs[2 * pieces :]
    q_s, k_s, v_s, o_s, do_s, dq_s, dk_s, dv_s, sems = refs
    nq = q_s.shape[0] // blk
    rows = per * blk
    take([q_ref], q_s, sems.at[0], blk, lambda i: place_ref[i])
    take([o_ref], o_s, sems.at[1], blk, lambda i: place_ref[i])
    take([do_ref], do_s, sems.at[2], blk, lambda i: place_ref[i])
    take(k_refs, k_s, sems.at[3], blk, lambda i: kslot_ref[i])
    take(v_refs, v_s, sems.at[4], blk, lambda i: kslot_ref[i])
    dk_s[...] = jnp.zeros_like(dk_s)
    dv_s[...] = jnp.zeros_like(dv_s)
    finish(q_s, sems.at[0])
    finish(o_s, sems.at[1])
    finish(do_s, sems.at[2])
    finish(k_s, sems.at[3])
    finish(v_s, sems.at[4])

    def tile_body(tile, carry):
        base = pl.multiple_of(tile * rows, rows)
        qpos = query_positions(seq_ref, tile, per, blk)
        full = (seq_ref[tile * per] * blk) // chunk
        last = ((seq_ref[tile * per + per - 1] + 1) * blk + chunk - 1) // chunk
        windows = [pl.ds(h * head_size, head_size) for h in range(heads)]
        qts = [q_s[pl.ds(base, rows), w] for w in windows]
        dos = [do_s[pl.ds(base, rows), w] for w in windows]
        deltas, lses = [], []
        for h, w in enumerate(windows):
            prod = dos[h].astype(jnp.float32) * o_s[pl.ds(base, rows), w].astype(jnp.float32)
            deltas.append(jnp.sum(prod.T, axis=0, keepdims=True))
            lses.append(lse_ref[pl.ds(tile * heads + h, 1), :])

        def step(j, accs, masked):
            low = pl.multiple_of(j * chunk, chunk)
            krows = pl.ds(low, chunk)
            if masked:
                kpos = low + lax.broadcasted_iota(jnp.int32, (chunk, rows), 0)
                seen = kpos <= qpos
            out = []
            for h, w in enumerate(windows):
                kc = k_s[krows, w]
                s = dot(kc, qts[h], 1, 1) * scale - lses[h]
                if masked:
                    s = jnp.where(seen, s, NEG)
                p = jnp.exp(s)
                dp = dot(v_s[krows, w], dos[h], 1, 1)
                ds = (p * (dp - deltas[h])).astype(jnp.bfloat16)
                dv_s[krows, w] += dot(p.astype(jnp.bfloat16), dos[h], 1, 0)
                dk_s[krows, w] += dot(ds, qts[h], 1, 0)
                out.append(accs[h] + dot(kc, ds, 0, 0))
            return tuple(out)

        accs = (jnp.zeros((head_size, rows), jnp.float32),) * heads
        accs = lax.fori_loop(0, full, functools.partial(step, masked=False), accs)
        accs = lax.fori_loop(full, last, functools.partial(step, masked=True), accs)
        for h, w in enumerate(windows):
            dq_s[pl.ds(base, rows), w] = (accs[h] * scale).T
        return carry

    lax.fori_loop(0, nq // per, tile_body, 0)
    v_s[...] = dv_s[...].astype(v_s.dtype)
    give(v_s, dv_refs, sems.at[4], blk, lambda i: kslot_ref[i])
    k_s[...] = (dk_s[...] * scale).astype(k_s.dtype)
    give(k_s, dk_refs, sems.at[3], blk, lambda i: kslot_ref[i])
    give(dq_s, [dq_ref], sems.at[0], blk, lambda i: place_ref[i])
    finish(v_s, sems.at[4])
    finish(k_s, sems.at[3])
    finish(dq_s, sems.at[0])


def attend_back(place, seq, kslot, q, ks, vs, o, do, lse, heads, head_size, blk):
    nq = q.shape[0] // blk
    per = min(4, nq)
    keys = sum(k.shape[0] for k in ks)
    bf16, f32 = q.dtype, jnp.float32
    out = pl.pallas_call(
        functools.partial(
            attend_back_kernel, heads=heads, head_size=head_size, blk=blk, per=per, chunk=512,
            scale=1.0 / math.sqrt(head_size), pieces=len(ks),
        ),
        out_shape=(
            jax.ShapeDtypeStruct(q.shape, f32),
            *(jax.ShapeDtypeStruct(k.shape, bf16) for k in ks),
            *(jax.ShapeDtypeStruct(v.shape, bf16) for v in vs),
        ),
        grid_spec=pltpu.PrefetchScalarGridSpec(
            num_scalar_prefetch=3,
            grid=(),
            in_specs=[ANY] * 3 + [WHOLE] + [ANY] * (2 * len(ks)),
            out_specs=[ANY] * (1 + 2 * len(ks)),
            scratch_shapes=[
                pltpu.VMEM(q.shape, bf16),
                pltpu.VMEM((keys, q.shape[1]), bf16),
                pltpu.VMEM((keys, q.shape[1]), bf16),
                pltpu.VMEM(q.shape, bf16),
                pltpu.VMEM(q.shape, bf16),
                pltpu.VMEM(q.shape, f32),
                pltpu.VMEM((keys, q.shape[1]), f32),
                pltpu.VMEM((keys, q.shape[1]), f32),
                pltpu.SemaphoreType.DMA((5,)),
            ],
        ),
        compiler_params=pltpu.CompilerParams(vmem_limit_bytes=60 * 1024 * 1024),
        name="attend_back",
    )(place, seq, kslot, q, o, do, lse, *ks, *vs)
    return out[0], out[1 : 1 + len(ks)], out[1 + len(ks) :]


def rotate(x, cosine, sine, heads, head_size):
    parts = []
    for h in range(heads):
        part = x[:, h * head_size : (h + 1) * head_size]
        parts.append(part * cosine + pltpu.roll(part, head_size // 2, 1) * sine)
    return jnp.concatenate(parts, axis=1)


def column(row):
    return jnp.broadcast_to(row, (8, row.shape[1])).T[:, :1]


def reciprocal_root(sums_ref, i, width):
    return column(lax.rsqrt(sums_ref[i : i + 1, :] / width + EPS))


def prepare_kernel(pre_ref, sums_ref, gain_ref, cos_ref, sin_ref, q_ref, k_ref, *, heads, head_size, width):
    wide = heads * head_size
    for i, out in enumerate((q_ref, k_ref)):
        recip = reciprocal_root(sums_ref, i, width)
        x = pre_ref[:, i * wide : (i + 1) * wide] * recip * gain_ref[i : i + 1, :]
        out[...] = rotate(x, cos_ref[...], sin_ref[...], heads, head_size).astype(out.dtype)


def by_row(step, n):
    return pl.BlockSpec((step, n), lambda i, *_: (i, 0))


def by_lane(step):
    return pl.BlockSpec((2, step), lambda i, *_: (0, i))


def fixed(rows, cols):
    return pl.BlockSpec((rows, cols), lambda i, *_: (0, 0))


TILE = 256


def prepare(pre, sums, gain, cosine, sine, heads, head_size, width):
    rows, wide = pre.shape[0], heads * head_size
    return pl.pallas_call(
        functools.partial(prepare_kernel, heads=heads, head_size=head_size, width=width),
        out_shape=(jax.ShapeDtypeStruct((rows, wide), jnp.bfloat16),) * 2,
        grid=(rows // TILE,),
        in_specs=[
            by_row(TILE, 2 * wide), by_lane(TILE), fixed(2, wide),
            by_row(TILE, head_size), by_row(TILE, head_size),
        ],
        out_specs=[by_row(TILE, wide)] * 2,
        name="prepare",
    )(pre, sums, gain, cosine, sine)


def unturn_kernel(
    dq_ref, dka_ref, dkb_ref, pre_ref, sums_ref, gain_ref, cos_ref, sin_ref,
    ds_ref, sum_ref, gg_ref, *, heads, head_size, width
):
    wide = heads * head_size
    dk = dka_ref[...] + dkb_ref[...].astype(jnp.float32)

    @pl.when(pl.program_id(0) == 0)
    def _():
        gg_ref[...] = jnp.zeros_like(gg_ref)

    for i, d in enumerate((dq_ref[...], dk)):
        cols = slice(i * wide, (i + 1) * wide)
        recip = reciprocal_root(sums_ref, i, width)
        n = rotate(d, cos_ref[...], -sin_ref[...], heads, head_size)
        pre = pre_ref[:, cols]
        gg_ref[i : i + 1, :] += jnp.sum(n * pre * recip, axis=0, keepdims=True)
        scaled = n * gain_ref[i : i + 1, :]
        ds_ref[:, cols] = scaled
        sum_ref[i : i + 1, :] = jnp.sum((scaled * pre).T, axis=0, keepdims=True)


def unturn(dq, dka, dkb, pre, sums, gain, cosine, sine, heads, head_size, width):
    rows, wide = pre.shape[0], heads * head_size
    return pl.pallas_call(
        functools.partial(unturn_kernel, heads=heads, head_size=head_size, width=width),
        out_shape=(
            jax.ShapeDtypeStruct((rows, 2 * wide), jnp.float32),
            jax.ShapeDtypeStruct((2, rows), jnp.float32),
            jax.ShapeDtypeStruct((2, wide), jnp.float32),
        ),
        grid=(rows // TILE,),
        in_specs=[
            by_row(TILE, wide), by_row(TILE, wide), by_row(TILE, wide), by_row(TILE, 2 * wide),
            by_lane(TILE), fixed(2, wide), by_row(TILE, head_size), by_row(TILE, head_size),
        ],
        out_specs=[by_row(TILE, 2 * wide), by_lane(TILE), fixed(2, wide)],
        name="unturn",
    )(dq, dka, dkb, pre, sums, gain, cosine, sine)


def fetch(refs, dst, sems):
    base = 0
    for ref in refs:
        rows = ref.shape[0]
        pltpu.make_async_copy(ref, dst.at[pl.ds(base, rows), :], sems.at[base // TILE]).start()
        base += rows


def arrive(dst, sems, tile):
    finish(dst.at[pl.ds(pl.multiple_of(tile * TILE, TILE), TILE), :], sems.at[tile])


def tile_rows(tile):
    return pl.ds(pl.multiple_of(tile * TILE, TILE), TILE)


def place_quarters(refs, dst, sem, cols, row_of):
    for j, ref in enumerate(refs):
        for s in range(ref.shape[0]):
            rows = ref.shape[1]
            row = pl.multiple_of(row_of(j // 2, j % 2, s) * rows, rows)
            pltpu.make_async_copy(ref.at[s, :, pl.ds(0, cols)], dst.at[pl.ds(row, rows), :], sem).start()


def project_kernel(me_ref, *refs, wide):
    x_refs, w_refs, refs = refs[:8], refs[8:12], refs[12:]
    pre_ref, v_ref, sum_ref, w_ref, x_s, x_sems, w_sem = refs
    tile = pl.program_id(0)

    @pl.when(tile == 0)
    def _():
        place_quarters(
            w_refs, w_ref, w_sem, 3 * wide,
            lambda jx, jy, s: (((s // 2) * 2 + (jy ^ me_ref[0])) * 2 + s % 2) * 2 + (jx ^ me_ref[1]),
        )
        fetch(x_refs, x_s, x_sems)
        finish(w_ref, w_sem)

    arrive(x_s, x_sems, tile)
    p = dot(x_s[tile_rows(tile), :], w_ref[...], 1, 0)
    pre_ref[...] = p[:, : 2 * wide]
    v_ref[...] = p[:, 2 * wide :].astype(v_ref.dtype)
    for i in range(2):
        part = p[:, i * wide : (i + 1) * wide]
        sum_ref[i : i + 1, :] = jnp.sum((part * part).T, axis=0, keepdims=True)


def project(me, xs, ws, wide):
    rows, d = xs[0].shape[0] * 8, xs[0].shape[1]
    bf16, f32 = xs[0].dtype, jnp.float32
    return pl.pallas_call(
        functools.partial(project_kernel, wide=wide),
        out_shape=(
            jax.ShapeDtypeStruct((rows, 2 * wide), f32),
            jax.ShapeDtypeStruct((rows, wide), bf16),
            jax.ShapeDtypeStruct((2, rows), f32),
            jax.ShapeDtypeStruct((d, 3 * wide), bf16),
        ),
        grid_spec=pltpu.PrefetchScalarGridSpec(
            num_scalar_prefetch=1,
            grid=(rows // TILE,),
            in_specs=[ANY] * 12,
            out_specs=[by_row(TILE, 2 * wide), by_row(TILE, wide), by_lane(TILE), fixed(d, 3 * wide)],
            scratch_shapes=[
                pltpu.VMEM((rows, d), bf16),
                pltpu.SemaphoreType.DMA((rows // TILE,)),
                pltpu.SemaphoreType.DMA,
            ],
        ),
        name="project",
    )(me, *xs, *ws)


def halves(tile, tiles, part, mine_ref, send_ref):
    @pl.when(tile < tiles // 2)
    def _():
        mine_ref[...] = part

    @pl.when(tile >= tiles // 2)
    def _():
        send_ref[...] = part.astype(send_ref.dtype)


def half_specs(tiles, cols):
    half = tiles // 2
    return [
        pl.BlockSpec((TILE, cols), lambda i, *_: (jnp.minimum(i, half - 1), 0)),
        pl.BlockSpec((TILE, cols), lambda i, *_: (jnp.maximum(i - half, 0), 0)),
    ]


def half_shapes(rows, cols):
    return [
        jax.ShapeDtypeStruct((rows // 2, cols), jnp.float32),
        jax.ShapeDtypeStruct((rows // 2, cols), jnp.bfloat16),
    ]


def expand_kernel(me_ref, *refs, units, tiles):
    x_refs, w_refs, d_refs, refs = refs[:8], refs[8:12], refs[12:16], refs[16:]
    gu_ref, hid_ref, mine_ref, send_ref, w_ref, d_ref, x_s, x_sems, w_sems = refs
    tile = pl.program_id(0)

    @pl.when(tile == 0)
    def _():
        place_quarters(
            w_refs, w_ref, w_sems.at[0], 2 * units,
            lambda jx, jh, s: (((s // 8) * 2 + (jh ^ me_ref[0])) * 8 + s % 8) * 2 + (jx ^ me_ref[1]),
        )
        fetch(x_refs, x_s, x_sems)
        place_quarters(
            d_refs, d_ref, w_sems.at[1], d_ref.shape[1],
            lambda jx, jh, s: (s * 2 + (jh ^ me_ref[0])) * 2 + (jx ^ me_ref[1]),
        )
        finish(w_ref, w_sems.at[0])

    arrive(x_s, x_sems, tile)
    p = dot(x_s[tile_rows(tile), :], w_ref[...], 1, 0)
    gu_ref[...] = p
    gate = p[:, :units]
    hidden = (gate * jax.nn.sigmoid(gate) * p[:, units:]).astype(hid_ref.dtype)
    hid_ref[...] = hidden

    @pl.when(tile == 0)
    def _():
        finish(d_ref, w_sems.at[1])

    halves(tile, tiles, dot(hidden, d_ref[...], 1, 0), mine_ref, send_ref)


def expand(me, xs, ws, ds, units):
    rows, d = xs[0].shape[0] * 8, xs[0].shape[1]
    tiles = rows // TILE
    bf16, f32 = xs[0].dtype, jnp.float32
    return pl.pallas_call(
        functools.partial(expand_kernel, units=units, tiles=tiles),
        out_shape=(
            jax.ShapeDtypeStruct((rows, 2 * units), f32),
            jax.ShapeDtypeStruct((rows, units), bf16),
            *half_shapes(rows, d),
            jax.ShapeDtypeStruct((d, 2 * units), bf16),
            jax.ShapeDtypeStruct((units, d), bf16),
        ),
        grid_spec=pltpu.PrefetchScalarGridSpec(
            num_scalar_prefetch=1,
            grid=(tiles,),
            in_specs=[ANY] * 16,
            out_specs=[
                by_row(TILE, 2 * units), by_row(TILE, units), *half_specs(tiles, d),
                fixed(d, 2 * units), fixed(units, d),
            ],
            scratch_shapes=[
                pltpu.VMEM((rows, d), bf16),
                pltpu.SemaphoreType.DMA((tiles,)),
                pltpu.SemaphoreType.DMA((2,)),
            ],
        ),
        name="expand",
    )(me, *xs, *ws, *ds)


def contract_kernel(gu_ref, w_ref, d_ref, *refs, units, tiles):
    x_refs, refs = refs[:8], refs[8:]
    dgu_ref, mine_ref, send_ref, x_s, x_sems = refs
    tile = pl.program_id(0)

    @pl.when(tile == 0)
    def _():
        fetch(x_refs, x_s, x_sems)

    arrive(x_s, x_sems, tile)
    dh = dot(x_s[tile_rows(tile), :], d_ref[...], 1, 1)
    gate, up = gu_ref[:, :units], gu_ref[:, units:]
    sig = jax.nn.sigmoid(gate)
    d_gate = (dh * up * sig * (1.0 + gate * (1.0 - sig))).astype(dgu_ref.dtype)
    d_up = (dh * (gate * sig)).astype(dgu_ref.dtype)
    dgu_ref[:, :units] = d_gate
    dgu_ref[:, units:] = d_up
    part = dot(d_gate, w_ref[:, :units], 1, 1) + dot(d_up, w_ref[:, units:], 1, 1)
    halves(tile, tiles, part, mine_ref, send_ref)


def contract(gu, w_gu, w_d, xs):
    units, d = w_d.shape
    rows = gu.shape[0]
    tiles = rows // TILE
    bf16 = w_d.dtype
    return pl.pallas_call(
        functools.partial(contract_kernel, units=units, tiles=tiles),
        out_shape=(jax.ShapeDtypeStruct((rows, 2 * units), bf16), *half_shapes(rows, d)),
        grid=(tiles,),
        in_specs=[by_row(TILE, 2 * units), fixed(d, 2 * units), fixed(units, d)] + [ANY] * 8,
        out_specs=[by_row(TILE, 2 * units), *half_specs(tiles, d)],
        scratch_shapes=[pltpu.VMEM((rows, d), bf16), pltpu.SemaphoreType.DMA((tiles,))],
        name="contract",
    )(gu, w_gu, w_d, *xs)


def outer_halves(a, b, me, keep_ref, send_ref):
    half = a.shape[1] // 2
    window = lambda i: a[:, pl.ds(pl.multiple_of(i * half, half), half)]
    keep_ref[...] = dot(window(me), b[...], 0, 0)
    send_ref[...] = dot(window(1 - me), b[...], 0, 0).astype(send_ref.dtype)


def grads_kernel(me_ref, hid_ref, dgu_ref, *refs):
    x_refs, g_refs, refs = refs[:8], refs[8:16], refs[16:]
    keep_gu, send_gu, keep_d, send_d, x_s, g_s, sems = refs
    base = 0
    for x_ref, g_ref in zip(x_refs, g_refs):
        rows = x_ref.shape[0]
        pltpu.make_async_copy(x_ref, x_s.at[pl.ds(base, rows), :], sems.at[0]).start()
        pltpu.make_async_copy(g_ref, g_s.at[pl.ds(base, rows), :], sems.at[1]).start()
        base += rows
    finish(x_s, sems.at[0])
    outer_halves(x_s, dgu_ref, me_ref[0], keep_gu, send_gu)
    finish(g_s, sems.at[1])
    outer_halves(hid_ref, g_s, me_ref[0], keep_d, send_d)


def split_shapes(rows, cols):
    return [
        jax.ShapeDtypeStruct((rows // 2, cols), jnp.float32),
        jax.ShapeDtypeStruct((rows // 2, cols), jnp.bfloat16),
    ]


def grads(me, hidden, d_gu, xs, gs):
    rows, units = hidden.shape
    d = xs[0].shape[1]
    bf16 = hidden.dtype
    return pl.pallas_call(
        grads_kernel,
        out_shape=(*split_shapes(d, 2 * units), *split_shapes(units, d)),
        grid_spec=pltpu.PrefetchScalarGridSpec(
            num_scalar_prefetch=1,
            grid=(),
            in_specs=[WHOLE, WHOLE] + [ANY] * 16,
            out_specs=[WHOLE] * 4,
            scratch_shapes=[
                pltpu.VMEM((rows, d), bf16),
                pltpu.VMEM((rows, d), bf16),
                pltpu.SemaphoreType.DMA((2,)),
            ],
        ),
        compiler_params=pltpu.CompilerParams(vmem_limit_bytes=40 * 1024 * 1024),
        name="grads",
    )(me, hidden, d_gu, *xs, *gs)


def project_back_kernel(me_ref, o_ref, w_ref, *refs):
    g_refs, refs = refs[:8], refs[8:]
    do_ref, keep_ref, send_ref, g_s, sem = refs
    base = 0
    for g_ref in g_refs:
        pltpu.make_async_copy(g_ref, g_s.at[pl.ds(base, g_ref.shape[0]), :], sem).start()
        base += g_ref.shape[0]
    finish(g_s, sem)
    do_ref[...] = dot(g_s[...], w_ref[...], 1, 1).astype(do_ref.dtype)
    outer_halves(o_ref, g_s, me_ref[0], keep_ref, send_ref)


def project_back(me, attended, w_o, gs):
    rows, wide = attended.shape
    d = w_o.shape[1]
    bf16 = w_o.dtype
    return pl.pallas_call(
        project_back_kernel,
        out_shape=(jax.ShapeDtypeStruct((rows, wide), bf16), *split_shapes(wide, d)),
        grid_spec=pltpu.PrefetchScalarGridSpec(
            num_scalar_prefetch=1,
            grid=(),
            in_specs=[WHOLE, WHOLE] + [ANY] * 8,
            out_specs=[WHOLE] * 3,
            scratch_shapes=[pltpu.VMEM((rows, d), bf16), pltpu.SemaphoreType.DMA],
        ),
        name="project_back",
    )(me, attended, w_o, *gs)


def norms_back_kernel(
    me_ref, ds_ref, sums_ref, dsums_ref, pre_ref, dva_ref, dvb_ref, *refs, wide, width, tiles
):
    x_refs, refs = refs[:8], refs[8:]
    dqkv_ref, keep_ref, send_ref, x_s, acc_s, x_sems = refs
    tile = pl.program_id(0)

    @pl.when(tile == 0)
    def _():
        fetch(x_refs, x_s, x_sems)
        acc_s[...] = jnp.zeros_like(acc_s)

    for i in range(2):
        cols = slice(i * wide, (i + 1) * wide)
        recip = reciprocal_root(sums_ref, i, width)
        total = column(dsums_ref[i : i + 1, :])
        value = recip * ds_ref[:, cols] - pre_ref[:, cols] * (recip * recip * recip) * total / width
        dqkv_ref[:, cols] = value.astype(dqkv_ref.dtype)
    dv = dva_ref[...] + dvb_ref[...].astype(jnp.float32)
    dqkv_ref[:, 2 * wide :] = dv.astype(dqkv_ref.dtype)
    arrive(x_s, x_sems, tile)
    acc_s[...] += dot(x_s[tile_rows(tile), :], dqkv_ref[...], 0, 0)

    @pl.when(tile == tiles - 1)
    def _():
        half = acc_s.shape[0] // 2
        window = lambda i: acc_s[pl.ds(pl.multiple_of(i * half, half), half), :]
        keep_ref[...] = window(me_ref[0])
        send_ref[...] = window(1 - me_ref[0]).astype(send_ref.dtype)


def norms_back(me, d_scaled, sums, dsums, pre, dva, dvb, xs, width):
    rows, wide = dva.shape
    d = xs[0].shape[1]
    tiles = rows // TILE
    bf16 = jnp.bfloat16
    half = d // 2
    return pl.pallas_call(
        functools.partial(norms_back_kernel, wide=wide, width=width, tiles=tiles),
        out_shape=(jax.ShapeDtypeStruct((rows, 3 * wide), bf16), *split_shapes(d, 3 * wide)),
        grid_spec=pltpu.PrefetchScalarGridSpec(
            num_scalar_prefetch=1,
            grid=(tiles,),
            in_specs=[
                by_row(TILE, 2 * wide), by_lane(TILE), by_lane(TILE), by_row(TILE, 2 * wide),
                by_row(TILE, wide), by_row(TILE, wide),
            ] + [ANY] * 8,
            out_specs=[by_row(TILE, 3 * wide), fixed(half, 3 * wide), fixed(half, 3 * wide)],
            scratch_shapes=[
                pltpu.VMEM((rows, d), bf16),
                pltpu.VMEM((d, 3 * wide), jnp.float32),
                pltpu.SemaphoreType.DMA((tiles,)),
            ],
        ),
        name="norms_back",
    )(me, d_scaled, sums, dsums, pre, dva, dvb, *xs)


def inputs_back_kernel(g_ref, w_ref, mine_ref, send_ref, *, tiles):
    halves(pl.program_id(0), tiles, dot(g_ref[...], w_ref[...], 1, 1), mine_ref, send_ref)


def inputs_back(g, w):
    rows, cols = g.shape
    d = w.shape[0]
    tiles = rows // TILE
    return pl.pallas_call(
        functools.partial(inputs_back_kernel, tiles=tiles),
        out_shape=tuple(half_shapes(rows, d)),
        grid=(tiles,),
        in_specs=[by_row(TILE, cols), fixed(d, cols)],
        out_specs=half_specs(tiles, d),
        name="inputs_back",
    )(g, w)


def unpack_kernel(src_ref, *refs, plan, pieces, cover):
    outs = refs[: len(plan[0])]
    got, wide, in_sems, out_sems = refs[len(outs) :]

    def fetch(p):
        return pltpu.make_async_copy(src_ref.at[p], got.at[p % 2], in_sems.at[p % 2])

    def parts(p):
        copies = []
        for out, moves in zip(outs, plan[p]):
            for rows, cols, drow, dcol in moves:
                copies.append(
                    pltpu.make_async_copy(
                        wide.at[p % 2, pl.ds(*rows), pl.ds(*cols)],
                        out.at[pl.ds(drow, rows[1]), pl.ds(dcol, cols[1])],
                        out_sems.at[p % 2],
                    )
                )
        return copies

    def done(p):
        window = wide.at[p % 2, pl.ds(0, cover), :]
        pltpu.make_async_copy(window, window, out_sems.at[p % 2]).wait()

    fetch(0).start()
    for p in range(pieces):
        if p + 1 < pieces:
            fetch(p + 1).start()
        fetch(p).wait()
        if p >= 2:
            done(p - 2)
        wide[p % 2] = got[p % 2].astype(jnp.float32)
        for copy in parts(p):
            copy.start()
    for p in range(max(pieces - 2, 0), pieces):
        done(p)


def unpack(src, shapes, plan, cover):
    pieces, rows, cols = src.shape
    return pl.pallas_call(
        functools.partial(unpack_kernel, plan=plan, pieces=pieces, cover=cover),
        out_shape=tuple(jax.ShapeDtypeStruct(s, jnp.float32) for s in shapes),
        in_specs=[ANY],
        out_specs=[ANY] * len(shapes),
        scratch_shapes=[
            pltpu.VMEM((2, rows, cols), src.dtype),
            pltpu.VMEM((2, rows, cols), jnp.float32),
            pltpu.SemaphoreType.DMA((2,)),
            pltpu.SemaphoreType.DMA((2,)),
        ],
        compiler_params=pltpu.CompilerParams(vmem_limit_bytes=40 * 1024 * 1024),
        name="unpack",
    )(src)


THETA = 500000.0
HD = 128


def norm_forward(value, gain):
    recip = lax.rsqrt(jnp.mean(value * value, axis=-1, keepdims=True) + EPS)
    return (value * recip * gain, recip)


def norm_backward(value, recip, gain, grad_out):
    scaled = grad_out * gain
    width = value.shape[-1]
    grad_in = (
        recip * scaled
        - value * (recip * recip * recip) * jnp.sum(scaled * value, axis=-1, keepdims=True) / width
    )
    grad_gain = jnp.sum(grad_out * value * recip, axis=0)
    return (grad_in, grad_gain)


def flip(value, *axes):
    last = 2 ** len(axes) - 1
    return lax.ppermute(value, axes, [(i, i ^ last) for i in range(last + 1)])


def after(value, *others):
    return lax.optimization_barrier((value, others))[0]


def gather8(x, a, b):
    own = [x, flip(x, b), flip(x, a), flip(x, a, b)]
    return own + [flip(v, "c") for v in own]


def scatter8(own, send, a, b):
    f32, bf16 = jnp.float32, jnp.bfloat16
    own = (own + flip(send, "c").astype(f32)).reshape(4, own.shape[0] // 4, own.shape[1])
    out = own.astype(bf16)
    return (
        own[0]
        + flip(out[1], b).astype(f32)
        + flip(out[2], a).astype(f32)
        + flip(out[3], a, b).astype(f32)
    )


def sum8(x, a, b):
    t = x.reshape(2, 8, -1)
    for bit, name in ((4, "c"), (2, a), (1, b)):
        got = flip(t.reshape(16, -1), name).reshape(t.shape)
        t = t + jnp.concatenate([got[:, k ^ bit : (k ^ bit) + 1] for k in range(8)], axis=1)
    return t.reshape(x.shape)


def in_order(value, axis, name):
    return jnp.where(lax.axis_index(name) == 1, jnp.flip(value, axis), value)


def quarters(x, a, b):
    first = flip(x, a)
    return [x, first, flip(x, b), flip(first, b)]


def gather4(x, a, b):
    quad = jnp.stack(quarters(x, a, b)).reshape((2, 2) + x.shape)
    return in_order(in_order(quad, 1, a), 0, b)


def halve(x, name, gate=()):
    me = lax.axis_index(name)
    keep = lax.dynamic_index_in_dim(x, me, 0, keepdims=False)
    send = lax.dynamic_index_in_dim(x, 1 - me, 0, keepdims=False)
    got = after(flip(send.astype(jnp.bfloat16), name), gate)
    return keep.astype(jnp.float32) + got.astype(jnp.float32)


def layer(
    layer_input,
    grad_output,
    positions,
    w_query,
    w_key,
    w_value,
    w_out,
    w_gate,
    w_up,
    w_down,
    gain_query,
    gain_key,
    gain_attn,
    gain_mlp,
    *,
    outer,
):
    f32 = jnp.float32
    bf16 = jnp.bfloat16
    rows, d = layer_input.shape
    drows, e = w_query.shape
    f = w_gate.shape[1]
    blk = rows // 2
    devices = positions.shape[0] // rows
    teams = devices // 8
    every = ("o", "h", "l", "y", "c", "x")
    heads = e // HD
    mine = heads // 8
    wide = mine * HD
    index = {name: lax.axis_index(name) for name in every}

    def by_team(w):
        return w.reshape(drows, mine, 8, HD).transpose(2, 0, 1, 3).reshape(8, drows, wide)

    gains = jnp.concatenate([gain_query, gain_key, gain_attn, gain_mlp])
    n_gains = gains.shape[0]
    pad = drows * 128 - n_gains
    gains = jnp.pad(gains, (0, pad)).reshape(1, drows, 128)
    payload = jnp.concatenate(
        [by_team(w_query), by_team(w_key), by_team(w_value), jnp.broadcast_to(gains, (8, drows, 128))],
        axis=2,
    )
    payload = lax.all_to_all(payload, ("h", "l", "c"), 0, 0, tiled=True)
    w_pieces = quarters(payload, "y", "x")
    lines = -(-(n_gains) // 128)
    gains = jnp.stack([p[:, :lines, 3 * wide :].reshape(8, lines * 128) for p in w_pieces]).astype(f32)
    if outer > 1:
        w_pieces = [lax.all_gather(p, "o", axis=0, tiled=True) for p in w_pieces]
        gains = lax.all_gather(gains, "o", axis=0)
    gains = gains.reshape(outer, 2, 2, 8, lines * 128)
    gains = in_order(in_order(gains, 2, "y"), 1, "x").reshape(outer, 2, 2, 2, 2, 2, lines * 128)
    gains = gains.transpose(0, 3, 4, 2, 5, 1, 6).reshape(devices, lines * 128)
    e_own, d_own = e // devices, d // devices
    full_gq = gains[:, :e_own].reshape(e)
    full_gk = gains[:, e_own : 2 * e_own].reshape(e)
    full_ga = gains[:, 2 * e_own : 2 * e_own + d_own].reshape(1, d).astype(f32)
    full_gm = gains[:, 2 * e_own + d_own : 2 * e_own + 2 * d_own].reshape(1, d).astype(f32)
    team_a = index["h"] * 4 + index["l"] * 2 + index["c"]

    def own_gain(g):
        return lax.dynamic_index_in_dim(g.reshape(mine, 8, HD), team_a, 1, keepdims=False).reshape(wide)

    gain_qk = jnp.stack([own_gain(full_gq), own_gain(full_gk)]).astype(f32)

    if outer == 1:
        w_o = gather4(w_out, "h", "x").transpose(1, 0, 2, 3).reshape(wide, d)
        w_o = lax.ppermute(
            w_o, ("h", "l", "y"), [(i, 2 * (i % 4) + i // 4) for i in range(8)]
        )
    else:
        w_o = lax.all_gather(w_out, every, axis=0, tiled=True).reshape(mine, 8, HD, d)
        w_o = lax.dynamic_index_in_dim(w_o, team_a, 1, keepdims=False).reshape(wide, d)

    unit = f // (8 * outer * 2)
    units = outer * 2 * unit

    def by_unit(w):
        return w.reshape(drows, outer * 2, 8, unit).transpose(2, 0, 1, 3).reshape(8, drows, units)

    ff = after(jnp.concatenate([by_unit(w_gate), by_unit(w_up)], axis=2), payload)
    ff = lax.all_to_all(ff, ("l", "y", "c"), 0, 0, tiled=True)
    table = positions.reshape(outer, 2, 2, 2, 2, 2, rows)[..., ::blk] // blk
    for axis, name in enumerate(every):
        if name != "o":
            table = in_order(table, axis, name)
    kslot = table.transpose(0, 5, 3, 4, 1, 2, 6)
    qblocks = lax.dynamic_index_in_dim(kslot, index["o"], 0, keepdims=False)[0, 0].reshape(-1)
    kslot = kslot.reshape(-1)
    nq = qblocks.shape[0]
    place = jnp.sum((qblocks[None, :] < qblocks[:, None]).astype(jnp.int32), axis=1)
    seq = jnp.sum(
        jnp.where(place[None, :] == jnp.arange(nq)[:, None], qblocks[None, :], 0), axis=1
    ).astype(jnp.int32)
    group_pos = (qblocks[:, None] * blk + jnp.arange(blk, dtype=jnp.int32)[None, :]).reshape(-1)
    freqs = THETA ** (-(2.0 * jnp.arange(HD // 2, dtype=f32)) / HD)
    angles = group_pos.astype(f32)[:, None] * freqs[None, :]
    cosine, sine = jnp.cos(angles), jnp.sin(angles)
    cosine = jnp.concatenate([cosine, cosine], axis=1)
    sine = jnp.concatenate([-sine, sine], axis=1)

    me_yx = jnp.stack([index["y"], index["x"]]).astype(jnp.int32)
    me_hx = jnp.stack([index["h"], index["x"]]).astype(jnp.int32)
    me_x = me_yx[1:]
    xs = gather8(layer_input.astype(bf16), "h", "l")
    group = 8 * rows
    pre, value, squares, w_qkv = project(me_yx, xs, w_pieces, wide)
    squares = sum8(squares, "h", "l")
    ff = after(ff, squares)
    w_down = after(w_down[None], squares)
    f_pieces = quarters(ff, "h", "x")
    d_pieces = quarters(w_down, "h", "x")
    if outer > 1:
        f_pieces = [lax.all_gather(p, "o", axis=0, tiled=True) for p in f_pieces]
        d_pieces = [lax.all_gather(p, "o", axis=0, tiled=True) for p in d_pieces]
    query, key = prepare(pre, squares, gain_qk, cosine, sine, mine, HD, e)
    key_y, value_x = flip(key, "y"), flip(value, "x")
    keys = [key, key_y, flip(key, "x"), flip(key_y, "x")]
    values = [value, flip(value, "y"), value_x, flip(value_x, "y")]
    if outer > 1:
        keys = [lax.all_gather(jnp.stack(keys), "o", axis=0).reshape(-1, wide)]
        values = [lax.all_gather(jnp.stack(values), "o", axis=0).reshape(-1, wide)]
    query = after(query, f_pieces[1], d_pieces[1])
    attended, lse, own, send = attend(place, seq, kslot, query, keys, values, w_o, mine, HD, blk)
    proj = scatter8(own, send, "h", "l")
    attn_branch, a_recip = norm_forward(proj, full_ga)
    mid = layer_input + attn_branch

    ms = gather8(mid.astype(bf16), "l", "y")
    gate_up, hidden, own, send, w_gu, w_d = expand(me_hx, ms, f_pieces, d_pieces, units)
    down = scatter8(own, send, "l", "y")
    mlp_branch, m_recip = norm_forward(down, full_gm)
    output = mid + mlp_branch
    d_down_f, local_gm = norm_backward(down, m_recip, full_gm, grad_output)
    dgs = gather8(d_down_f.astype(bf16), "l", "y")
    d_gu, own, send = contract(gate_up, w_gu, w_d, dgs)
    d_mid = grad_output + scatter8(own, send, "l", "y")
    keep_gu, send_gu, keep_d, send_d = grads(me_x, hidden, d_gu, ms, dgs)

    ctx = ("o", "h", "l", "y", "c")

    def fold(part, a, gate=()):
        cols = part.shape[1]
        part = halve(part.reshape(2, -1, cols), a, gate)
        if outer > 1:
            part = lax.psum_scatter(
                part.astype(bf16).reshape(outer, -1, cols), "o", scatter_dimension=0, tiled=False
            )
        return part.astype(bf16)

    d_proj_f, local_ga = norm_backward(proj, a_recip, full_ga, d_mid)
    pgs = gather8(d_proj_f.astype(bf16), "h", "l")
    got_gu, got_d = after((flip(send_gu, "x"), flip(send_d, "x")), pgs)
    sum_gu, sum_d = keep_gu + got_gu.astype(f32), keep_d + got_d.astype(f32)
    d_att, keep_o, send_o = project_back(me_x, attended, w_o, pgs)
    d_att = after(d_att, sum_gu, sum_d)
    dq_rot, dk, dv = attend_back(
        place, seq, kslot, query, keys, values, attended, d_att, lse, mine, HD, blk
    )
    if outer > 1:
        def own_quarter(g):
            g = g[0].reshape(outer, 4, group, wide)
            return list(lax.psum_scatter(g, "o", scatter_dimension=0, tiled=False))

        dk, dv = own_quarter(dk), own_quarter(dv)
    dk_a = dk[0].astype(f32) + flip(dk[2], "x").astype(f32)
    dk_b = flip((dk[1].astype(f32) + flip(dk[3], "x").astype(f32)).astype(bf16), "y")
    dv_a = dv[0].astype(f32) + flip(dv[1], "y").astype(f32)
    dv_b = flip((dv[2].astype(f32) + flip(dv[3], "y").astype(f32)).astype(bf16), "x")
    d_scaled, dsums, local_gqk = unturn(
        dq_rot, dk_a, dk_b, pre, squares, gain_qk, cosine, sine, mine, HD, e
    )
    dsums = sum8(dsums, "h", "l")
    d_qkv, keep_qkv, send_qkv = norms_back(me_x, d_scaled, squares, dsums, pre, dv_a, dv_b, xs, e)
    own, send = inputs_back(d_qkv, w_qkv)
    grad_input = d_mid + scatter8(own, send, "h", "l")

    half_d, half_f = d // 2, f // 2
    part_gu, part_d = fold(sum_gu, "h", dq_rot), fold(sum_d, "h", dq_rot)
    part_o = fold(keep_o + flip(send_o, "x").astype(f32), "y")
    part_qkv = fold(keep_qkv + flip(send_qkv, "x").astype(f32), "y")
    n_qk, n_am = wide, d
    lines = -(-max(n_qk, n_am) // (3 * wide))
    lines = -(-lines // 16) * 16

    def line(v, n):
        return jnp.pad(v.reshape(2, n), ((0, 0), (0, lines * 3 * wide - n)))

    small = jnp.stack(
        [
            line(local_gqk.reshape(2, 2, -1).transpose(1, 0, 2), n_qk),
            line(jnp.stack([local_ga, local_gm]).reshape(2, 2, -1).transpose(1, 0, 2), n_am),
        ],
        axis=1,
    )
    small = halve(small, "x")
    small = halve(small, "y")
    if outer > 1:
        small = lax.psum(small, "o") / outer
    small = small.reshape(lines, 3 * wide).astype(bf16)
    part_qkv = jnp.concatenate([part_qkv, small])
    n_gu, n_d, n_o, n_qkv = part_gu.shape[0], part_d.shape[0], part_o.shape[0], part_qkv.shape[0] - lines

    if outer == 1:
        first = lax.all_gather(jnp.concatenate([part_gu, part_d, part_o]), ctx, axis=0).reshape(16, -1, d)
        part_qkv = after(part_qkv, first)
        last = lax.all_gather(part_qkv, ctx, axis=0).reshape(16, -1, 3 * wide)
        plan_first, plan_last = [], []
        for p in range(16):
            h, l, y, c = p >> 3, (p >> 2) & 1, (p >> 1) & 1, p & 1
            team_f, team_q = 4 * l + 2 * y + c, 4 * h + 2 * l + c
            ups = [
                [
                    ((0, n_gu), (m * units + o * unit, unit), h * n_gu, (o * 8 + team_f) * unit)
                    for o in range(2)
                ]
                for m in range(2)
            ]
            downs = [((n_gu, n_d), (0, d), team_f * unit + h * n_d, 0)]
            outs = [((n_gu + n_d, n_o), (0, d), team_q * HD + y * n_o, 0)]
            plan_first.append([*ups, downs, outs])
            plan_last.append(
                [
                    [
                        ((0, n_qkv), (m * wide + o * HD, HD), y * n_qkv, (o * 8 + team_q) * HD)
                        for o in range(mine)
                    ]
                    for m in range(3)
                ]
            )
        total_wg, total_wu, total_wd, total_wo = unpack(
            first, [(half_d, f), (half_d, f), (half_f, d), (e // 2, d)], plan_first, n_gu + n_d + n_o
        )
        total_wq, total_wk, total_wv = unpack(last, [(half_d, e)] * 3, plan_last, n_qkv)
        got_small = last[:, n_qkv:]
    else:
        got = lax.all_gather(part_qkv, ctx, axis=0)
        got_small = got.reshape(-1, n_qkv + lines, 3 * wide)[:, n_qkv:]
        got = got.reshape(outer, 2, 2, 2, 2, n_qkv + lines, 3 * wide)[..., :n_qkv, :]
        got = got.transpose(3, 0, 5, 1, 2, 4, 6).reshape(half_d, 8, 3, mine, HD)
        got = got.transpose(2, 0, 3, 1, 4).reshape(3, half_d, e)
        total_wq, total_wk, total_wv = got[0].astype(f32), got[1].astype(f32), got[2].astype(f32)
        got = lax.all_gather(part_gu, ctx, axis=0)
        got = got.reshape(outer, 2, 8, n_gu, 2, outer * 2, unit)
        got = got.transpose(4, 1, 0, 3, 5, 2, 6).reshape(2, half_d, f)
        total_wg, total_wu = got[0].astype(f32), got[1].astype(f32)
        got = lax.all_gather(part_d, ctx, axis=0)
        got = got.reshape(outer, 2, 8, n_d, d).transpose(2, 1, 0, 3, 4)
        total_wd = got.reshape(8, outer, unit, d).transpose(1, 0, 2, 3).reshape(half_f, d).astype(f32)
        got = lax.all_gather(part_o, ctx, axis=0)
        got = got.reshape(outer, 2, 2, 2, 2, n_o, d).transpose(1, 2, 4, 3, 0, 5, 6)
        total_wo = got.reshape(e // 2, d).astype(f32)

    got_small = got_small.astype(f32).reshape(outer, 4, 2, 2, lines * 3 * wide)
    if outer > 1:
        got_small = jnp.sum(got_small, axis=0)
    else:
        got_small = got_small[0]
    qk = got_small[:, 0, :, :n_qk].reshape(8, 2, mine // 2, HD).transpose(1, 2, 0, 3).reshape(2, e // 2)
    total_gq, total_gk = qk[0], qk[1]
    am = jnp.sum(got_small[:, 1, :, :n_am], axis=(0, 1)).reshape(2, half_d)
    total_ga, total_gm = am[0], am[1]
    return (
        output,
        grad_input,
        total_wq,
        total_wk,
        total_wv,
        total_wo,
        total_wg,
        total_wu,
        total_wd,
        total_gq,
        total_gk,
        total_ga,
        total_gm,
    )


def solution(mesh):
    outer = mesh.shape["ctx"] // 16
    names = ("o", "h", "l", "y", "c", "x")
    fine = Mesh(mesh.devices.reshape(outer, 2, 2, 2, 2, 2), names)
    every, half = P(names), P("x")
    in_specs = (every, every, P()) + (every,) * 11
    out_specs = (every, every) + (half,) * 11
    return jax.shard_map(
        functools.partial(layer, outer=outer),
        mesh=fine,
        in_specs=in_specs,
        out_specs=out_specs,
        check_vma=False,
    )
```
